32 devices in a mesh: group: 2 (over x), circ: 16 (over z, y, core).
Axes of the slice: x: 2, y: 2, z: 4, core: 2. Of those that a mesh axis runs over, the one named last changes fastest.
Arguments:
- state_field: float32 [6, 256, 515], P('group', 'circ'), parts along dimension 0, may hold values from -3 to 3
- direction: float32 [6, 256, 515], P('group', 'circ'), parts along dimension 0, may hold values from -6 to 6
- skin_thickness: float32 [256, 515], P('circ'), may hold values from 0.2 to 3
- stringer_column: int32 [16], P('circ'), may hold values from 0 to 253, as said below
Outputs:
- lanczos_vectors: float32 [6, 3, 256, 515], P('group', None, 'circ'), parts along dimension 0
- lanczos_diagonal: float32 [6], P('group'), parts along dimension 0
- lanczos_subdiagonal: float32 [6], P('group'), parts along dimension 0
The draws below stay inside these ranges and needn't reach their ends.
There are 2 independent parts, one for each index of `group`. The reference program is written for one: setup_inputs(seed, part) draws one part's arguments, and reference() takes and returns one part's arrays. A program takes and returns all parts, laid end to end along the dimension named above; an argument that names none is the same for every part. Nothing has to cross between parts.
Inputs may be any that keep to these rules, and one draw needn't show every extreme that they name: `stringer_column`: stringer k is attached at the start of span c with k * 16 <= c <= (k + 1) * 16 - 3.
All inputs are finite; a program needn't handle non-finite values.
Results may differ from the reference program's by a relative error of at most 0.0003.
Values sent between devices are 32-bit elements; how exact they have to be, the bound alone decides.
No kernel may reach another device: no remote copies, remote signals or barrier semaphores. Data moves between devices by JAX's collectives and lax.ppermute only.
A program may use at most 64 MiB of HBM per device.

```python
import math
import jax
import jax.numpy as jnp
from jax import lax

STEPS = 3
NA = 515
NC = 256
GAP = 16
STRINGERS = 16


def draw_skin_thickness(key, part):
    columns = jnp.arange(NC, dtype=jnp.float32)[:, None] / NC
    rising = 0.5 * jnp.exp(jnp.log(3.0) * columns)
    rough = jnp.exp(jax.random.uniform(key, (NC, NA), jnp.float32, -0.35, 0.35))
    return rising * rough


def draw_stringer_column(key, part):
    offsets = jax.random.randint(key, (STRINGERS,), 0, GAP - 2, dtype=jnp.int32)
    offsets = offsets.at[0].set(0).at[STRINGERS - 1].set(GAP - 3)
    return jnp.arange(STRINGERS, dtype=jnp.int32) * GAP + offsets


def block_levels(stream_key, dims, shards, low, high):
    loudness, own = 1.0, jax.random.fold_in(stream_key, 6)
    for position, blocks in shards:
        steps = jnp.exp(jax.random.uniform(jax.random.fold_in(own, position), (blocks,), jnp.float32, low / len(shards), high / len(shards)))
        loudness = loudness * jnp.repeat(steps, dims[position] // blocks).reshape([-1 if axis == position else 1 for axis in range(len(dims))])
    return loudness


def scatter_about(stream_key, extent, scale, reach, pieces=(), kind=jnp.bfloat16):
    values = jax.random.normal(stream_key, extent, jnp.float32) * scale
    if len(pieces) > 0:
        values = block_levels(stream_key, extent, pieces, -0.22, 0.18) * values
    return jnp.clip(values, min=-reach, max=reach).astype(kind)


def setup_inputs(seed: int = 0, part: int = 0) -> dict:
    splits = jax.random.split(jax.random.key(seed), 5)
    own_keys = jax.random.split(jax.random.fold_in(splits[4], part), 5)
    state_field = scatter_about(own_keys[0], (3, NC, NA), 0.5, 3.0, ((1, 16),), jnp.float32)
    direction = scatter_about(own_keys[1], (3, NC, NA), 1.0, 6.0, ((1, 16),), jnp.float32)
    skin_thickness = draw_skin_thickness(jax.random.fold_in(splits[4], 71), part)
    stringer_column = draw_stringer_column(jax.random.fold_in(splits[4], 71), part)
    return {"state_field": state_field, "direction": direction, "skin_thickness": skin_thickness, "stringer_column": stringer_column}


POISSON = 0.3
EPSILON = 1e-06
STRINGER_AXIAL = 40.0
STRINGER_BENDING = 20.0
END_STIFF = 4.0

def gauss_rule():
    inner_root = math.sqrt(3.0 / 7.0 - 2.0 / 7.0 * math.sqrt(6.0 / 5.0))
    outer_root = math.sqrt(3.0 / 7.0 + 2.0 / 7.0 * math.sqrt(6.0 / 5.0))
    weight_inner = (18.0 + math.sqrt(30.0)) / 72.0
    weight_outer = (18.0 - math.sqrt(30.0)) / 72.0
    points = [0.5 - 0.5 * outer_root, 0.5 - 0.5 * inner_root, 0.5 + 0.5 * inner_root, 0.5 + 0.5 * outer_root]
    weights = [weight_outer, weight_inner, weight_inner, weight_outer]
    return (points, weights)

def basis_value(degree, offset, location):
    other_side = 1.0 - location
    if degree == 0:
        values = [other_side ** 3 / 6.0, (3.0 * location ** 3 - 6.0 * location ** 2 + 4.0) / 6.0, (-3.0 * location ** 3 + 3.0 * location ** 2 + 3.0 * location + 1.0) / 6.0, location ** 3 / 6.0]
    elif degree == 1:
        values = [-other_side ** 2 / 2.0, 1.5 * location ** 2 - 2.0 * location, -1.5 * location ** 2 + location + 0.5, location ** 2 / 2.0]
    else:
        values = [other_side, 3.0 * location - 2.0, 1.0 - 3.0 * location, location]
    return values[offset]

def spline_table():
    points, weights = gauss_rule()
    spline_rows = []
    for degree in range(3):
        row_list = []
        for offset in range(4):
            row_list.append([basis_value(degree, offset, location) for location in points])
        spline_rows.append(row_list)
    return (spline_rows, weights)

def axial_take(values, degree, axial_point, spline_rows):
    elements = values.shape[-1] - 3
    summed = spline_rows[degree][0][axial_point] * values[..., 0:elements]
    for offset in range(1, 4):
        summed = summed + spline_rows[degree][offset][axial_point] * values[..., offset:offset + elements]
    return summed

def axial_put(values, degree, axial_point, spline_rows, weight):
    summed = 0.0
    for offset in range(4):
        pad_widths = [(0, 0)] * (values.ndim - 1) + [(offset, 3 - offset)]
        summed = summed + jnp.pad(spline_rows[degree][offset][axial_point] * weight * values, pad_widths)
    return summed

def circ_take(values, degree, circ_point, spline_rows):
    summed = spline_rows[degree][0][circ_point] * values
    for offset in range(1, 4):
        summed = summed + spline_rows[degree][offset][circ_point] * jnp.roll(values, -offset, axis=-2)
    return summed

def circ_put(term_pairs, circ_point, spline_rows, weight):
    summed = 0.0
    for offset in range(4):
        combined = 0.0
        for degree, values in term_pairs:
            combined = combined + spline_rows[degree][offset][circ_point] * values
        summed = summed + jnp.roll(weight * combined, offset, axis=-2)
    return summed

def membrane_forces(strain_axial, strain_circ, strain_shear, stiffness):
    return (stiffness * (strain_axial + POISSON * strain_circ), stiffness * (POISSON * strain_axial + strain_circ), stiffness * 0.5 * (1.0 - POISSON) * strain_shear)

def state_point(state_zero, state_one, thick_zero, circ_point, spline_rows, radius):
    axial_along = circ_take(state_one[0], 0, circ_point, spline_rows)
    axial_across = circ_take(state_zero[0], 1, circ_point, spline_rows)
    circ_across = circ_take(state_zero[1], 1, circ_point, spline_rows)
    circ_along = circ_take(state_one[1], 0, circ_point, spline_rows)
    deflect = circ_take(state_zero[2], 0, circ_point, spline_rows)
    deflect_along = circ_take(state_one[2], 0, circ_point, spline_rows)
    deflect_across = circ_take(state_zero[2], 1, circ_point, spline_rows)
    thickness = circ_take(thick_zero, 0, circ_point, spline_rows)
    inverse = 1.0 / (1.0 - POISSON * POISSON)
    membrane = inverse * thickness
    bending = inverse * thickness ** 3 / 12.0
    strain_axial = axial_along + 0.5 * deflect_along ** 2
    strain_circ = circ_across + deflect / radius + 0.5 * deflect_across ** 2
    strain_shear = axial_across + circ_along + deflect_along * deflect_across
    forces = membrane_forces(strain_axial, strain_circ, strain_shear, membrane)
    return (deflect_along, deflect_across) + forces + (membrane, bending)

def point_pairs(state_set, vector_zero, vector_one, vector_two, circ_point, spline_rows, radius):
    deflect_along, deflect_across, force_axial, force_circ, force_shear, membrane, bending = state_set
    delta_axial_along = circ_take(vector_one[0], 0, circ_point, spline_rows)
    delta_axial_across = circ_take(vector_zero[0], 1, circ_point, spline_rows)
    delta_circ_across = circ_take(vector_zero[1], 1, circ_point, spline_rows)
    delta_circ_along = circ_take(vector_one[1], 0, circ_point, spline_rows)
    delta_deflect = circ_take(vector_zero[2], 0, circ_point, spline_rows)
    delta_slope_along = circ_take(vector_one[2], 0, circ_point, spline_rows)
    delta_slope_across = circ_take(vector_zero[2], 1, circ_point, spline_rows)
    delta_curve_along = circ_take(vector_two, 0, circ_point, spline_rows)
    delta_curve_across = circ_take(vector_zero[2], 2, circ_point, spline_rows)
    delta_twist = circ_take(vector_one[2], 1, circ_point, spline_rows)
    strain_axial = delta_axial_along + deflect_along * delta_slope_along
    strain_circ = delta_circ_across + delta_deflect / radius + deflect_across * delta_slope_across
    strain_shear = delta_axial_across + delta_circ_along + deflect_along * delta_slope_across + deflect_across * delta_slope_along
    axial_force, circ_force, shear_force = membrane_forces(strain_axial, strain_circ, strain_shear, membrane)
    axial_moment, circ_moment, twist_moment = membrane_forces(-delta_curve_along, -delta_curve_across, -2.0 * delta_twist, bending)
    slope_along = axial_force * deflect_along + shear_force * deflect_across + force_axial * delta_slope_along + force_shear * delta_slope_across
    slope_across = circ_force * deflect_across + shear_force * deflect_along + force_circ * delta_slope_across + force_shear * delta_slope_along
    return {(0, 1): [(0, axial_force)], (0, 0): [(1, shear_force)], (1, 0): [(1, circ_force)], (1, 1): [(0, shear_force)], (2, 0): [(0, circ_force / radius), (1, slope_across), (2, -circ_moment)], (2, 1): [(0, slope_along), (1, -2.0 * twist_moment)], (2, 2): [(0, -axial_moment)]}

def skin_product(state_field, thick_field, vector_field, radius, spline_rows, weights):
    comp_totals = [0.0, 0.0, 0.0]
    for axial_point in range(4):
        state_zero = axial_take(state_field, 0, axial_point, spline_rows)
        state_one = axial_take(state_field, 1, axial_point, spline_rows)
        thick_zero = axial_take(thick_field, 0, axial_point, spline_rows)
        vector_zero = axial_take(vector_field, 0, axial_point, spline_rows)
        vector_one = axial_take(vector_field, 1, axial_point, spline_rows)
        vector_two = axial_take(vector_field[2], 2, axial_point, spline_rows)
        holders = {}
        for circ_point in range(4):
            state_set = state_point(state_zero, state_one, thick_zero, circ_point, spline_rows, radius)
            pair_map = point_pairs(state_set, vector_zero, vector_one, vector_two, circ_point, spline_rows, radius)
            for slot_pair in sorted(pair_map):
                added = circ_put(pair_map[slot_pair], circ_point, spline_rows, weights[circ_point])
                holders[slot_pair] = holders[slot_pair] + added if slot_pair in holders else added
        for slot_pair in sorted(holders):
            component = slot_pair[0]
            comp_totals[component] = comp_totals[component] + axial_put(holders[slot_pair], slot_pair[1], axial_point, spline_rows, weights[axial_point])
    return jnp.stack(comp_totals)

def placement_matrix(attach, columns):
    offset_diff = columns[None, :] - attach[:, None]
    return (jnp.where(offset_diff == 0, 1.0 / 6.0, 0.0) + jnp.where(offset_diff == 1, 4.0 / 6.0, 0.0) + jnp.where(offset_diff == 2, 1.0 / 6.0, 0.0)).astype(jnp.float32)

def stringer_state(state_field, placement, spline_rows):
    line_fields = jnp.einsum('kc,ica->ika', placement, jnp.stack([state_field[0], state_field[2]]), precision=lax.Precision.HIGHEST)
    return [(axial_take(line_fields[0], 1, axial_point, spline_rows), axial_take(line_fields[1], 1, axial_point, spline_rows)) for axial_point in range(4)]

def stringer_product(stringer_points, vector_field, placement, spline_rows, weights):
    delta_lines = jnp.einsum('kc,ica->ika', placement, jnp.stack([vector_field[0], vector_field[2]]), precision=lax.Precision.HIGHEST)
    axial_total = 0.0
    deflect_total = 0.0
    for axial_point in range(4):
        line_along, line_slope = stringer_points[axial_point]
        delta_along = axial_take(delta_lines[0], 1, axial_point, spline_rows)
        delta_slope = axial_take(delta_lines[1], 1, axial_point, spline_rows)
        delta_curve = axial_take(delta_lines[1], 2, axial_point, spline_rows)
        stretch = line_along + 0.5 * line_slope ** 2
        delta_stretch = delta_along + line_slope * delta_slope
        weight = weights[axial_point]
        axial_total = axial_total + axial_put(STRINGER_AXIAL * delta_stretch, 1, axial_point, spline_rows, weight)
        deflect_total = deflect_total + axial_put(STRINGER_AXIAL * (delta_stretch * line_slope + stretch * delta_slope), 1, axial_point, spline_rows, weight) + axial_put(STRINGER_BENDING * delta_curve, 2, axial_point, spline_rows, weight)
    spread_back = jnp.einsum('kc,ika->ica', placement, jnp.stack([axial_total, deflect_total]), precision=lax.Precision.HIGHEST)
    return jnp.stack([spread_back[0], jnp.zeros_like(spread_back[0]), spread_back[1]])

def end_product(vector_field):
    kernel = jnp.array([1.0, 4.0, 1.0], jnp.float32) / 6.0
    first_row = END_STIFF * (vector_field[..., 0] + 4.0 * vector_field[..., 1] + vector_field[..., 2]) / 6.0
    last_row = END_STIFF * (vector_field[..., -3] + 4.0 * vector_field[..., -2] + vector_field[..., -1]) / 6.0
    length = vector_field.shape[-1]
    pad_lead = [(0, 0)] * (vector_field.ndim - 1)
    return jnp.pad(first_row[..., None] * kernel, pad_lead + [(0, length - 3)]) + jnp.pad(last_row[..., None] * kernel, pad_lead + [(length - 3, 0)])

def reference(state_field, direction, skin_thickness, stringer_column):
    spline_rows, weights = spline_table()
    radius = NC / (2.0 * math.pi)
    count_all = 3.0 * NC * NA
    placement = placement_matrix(stringer_column, jnp.arange(NC, dtype=jnp.int32))
    stringer_points = stringer_state(state_field, placement, spline_rows)

    def shell_operator(vector_field):
        skin_part = skin_product(state_field, skin_thickness, vector_field, radius, spline_rows, weights)
        return skin_part + stringer_product(stringer_points, vector_field, placement, spline_rows, weights) + end_product(vector_field)
    beta_first = jnp.sqrt(jnp.sum(direction * direction) / count_all + EPSILON)

    def lanczos_step(carry, unused):
        current, previous, beta_last = carry
        image_field = shell_operator(current)
        alpha_value = jnp.sum(current * image_field) / count_all
        residual_vec = image_field - alpha_value * current - beta_last * previous
        beta_value = jnp.sqrt(jnp.sum(residual_vec * residual_vec) / count_all + EPSILON)
        next_vec = residual_vec / beta_value
        return ((next_vec, current, beta_value), (next_vec, alpha_value, beta_value))
    start = (direction / beta_first, jnp.zeros_like(direction), beta_first)
    unused_carry, stacked = lax.scan(lanczos_step, start, None, length=STEPS)
    return (stacked[0], stacked[1], stacked[2])
```

```python
import functools
import math

import jax
import jax.numpy as jnp
from jax import lax
from jax.experimental import pallas as pl
from jax.experimental.pallas import tpu as pltpu
from jax.sharding import PartitionSpec as P

STEPS = 3

POISSON = 0.3
EPSILON = 1e-06
STRINGER_AXIAL = 40.0
STRINGER_BENDING = 20.0
END_STIFF = 4.0

LANES = 128
SUBS = 8
HALF = 4
HALO = 3 * STEPS

A1, B1, C0, C1, C2, DA0, DB0, DC0, DC1, DDC0, H0 = range(11)
F01, F00, F10, F11, F20, F20Q, F20L, F21, F21Q, F22 = range(10)
S_WX, S_WS, S_NX, S_NS, S_NG, S_A, S_AG, S_D = range(8)


def gauss_rule():
    inner_root = math.sqrt(3.0 / 7.0 - 2.0 / 7.0 * math.sqrt(6.0 / 5.0))
    outer_root = math.sqrt(3.0 / 7.0 + 2.0 / 7.0 * math.sqrt(6.0 / 5.0))
    weight_inner = (18.0 + math.sqrt(30.0)) / 72.0
    weight_outer = (18.0 - math.sqrt(30.0)) / 72.0
    points = [
        0.5 - 0.5 * outer_root,
        0.5 - 0.5 * inner_root,
        0.5 + 0.5 * inner_root,
        0.5 + 0.5 * outer_root,
    ]
    return points, [weight_outer, weight_inner, weight_inner, weight_outer]


def cubic(t):
    s = 1.0 - t
    return [
        s**3 / 6.0,
        (3.0 * t**3 - 6.0 * t**2 + 4.0) / 6.0,
        (-3.0 * t**3 + 3.0 * t**2 + 3.0 * t + 1.0) / 6.0,
        t**3 / 6.0,
    ]


def quadratic(t):
    return [(1.0 - t) ** 2 / 2.0, -(t**2) + t + 0.5, t**2 / 2.0]


POINTS, WEIGHTS = gauss_rule()


def take4(z):
    p03, m03, p12, m12 = z[0] + z[3], z[0] - z[3], z[1] + z[2], z[1] - z[2]

    def at(t, scale=1.0):
        b = [scale * x for x in cubic(t)]
        even = p03 * (0.5 * (b[0] + b[3])) + p12 * (0.5 * (b[1] + b[2]))
        odd = m03 * (0.5 * (b[0] - b[3])) + m12 * (0.5 * (b[1] - b[2]))
        return even, odd

    return at


def take3(d):
    p, m = d[0] + d[2], d[0] - d[2]

    def at(t, scale=1.0):
        q = [scale * x for x in quadratic(t)]
        return p * (0.5 * (q[0] + q[2])) + d[1] * q[1], m * (0.5 * (q[0] - q[2]))

    return at


def take2(g):
    even, m = 0.5 * (g[0] + g[1]), g[0] - g[1]

    def at(t):
        return even, m * (0.5 - t)

    return at


def both(pair):
    return pair[0] + pair[1], pair[0] - pair[1]


def merged(first, second):
    return first[0] + second[0], first[1] + second[1]


def put4(pairs, scale=1.0):
    sums = None
    for t, (one, two) in pairs:
        s, d = one + two, one - two
        b = [scale * x for x in cubic(t)]
        terms = [
            s * (0.5 * (b[0] + b[3])),
            d * (0.5 * (b[0] - b[3])),
            s * (0.5 * (b[1] + b[2])),
            d * (0.5 * (b[1] - b[2])),
        ]
        sums = terms if sums is None else [x + y for x, y in zip(sums, terms)]
    e03, o03, e12, o12 = sums
    return [e03 + o03, e12 + o12, e12 - o12, e03 - o03]


def put3(pairs):
    sums = None
    for t, (one, two) in pairs:
        s, d = one + two, one - two
        q = quadratic(t)
        terms = [s * (0.5 * (q[0] + q[2])), d * (0.5 * (q[0] - q[2])), s * q[1]]
        sums = terms if sums is None else [x + y for x, y in zip(sums, terms)]
    even, odd, middle = sums
    return [even + odd, middle, even - odd]


def put2(pairs):
    even, odd = None, None
    for t, (one, two) in pairs:
        s, d = one + two, (one - two) * (0.5 - t)
        even = s if even is None else even + s
        odd = d if odd is None else odd + d
    even = 0.5 * even
    return [even + odd, even - odd]


def krylov_kernel(
    own_cols,
    pad,
    radius,
    left_ref,
    own_ref,
    right_ref,
    krylov_ref,
    gram_ref,
    field_ref,
    take_ref,
    acc_ref,
    state_ref,
    image_ref,
    table_ref,
    line_ref,
):
    sub = lax.broadcasted_iota(jnp.int32, (SUBS, LANES), 0)
    lane = lax.broadcasted_iota(jnp.int32, (SUBS, LANES), 1)
    low = sub < HALF
    zero = jnp.zeros((SUBS, LANES), jnp.float32)

    for h in range(2):
        first, second = POINTS[h], POINTS[3 - h]
        rows = (
            list(zip(cubic(first), cubic(second)))
            + list(zip(quadratic(first), quadratic(second)))
            + [(1.0 - first, 1.0 - second), (first, second)]
        )
        for i, (x, y) in enumerate(rows):
            table_ref[h, i] = jnp.where(low, jnp.float32(x), jnp.float32(y))

    field_ref[...] = jnp.zeros_like(field_ref)
    chunks = left_ref.shape[2] // LANES
    for source, offset in (
        (left_ref, pad - HALO),
        (own_ref, pad),
        (right_ref, pad + own_cols),
    ):
        for i in range(source.shape[0]):
            for c in range(chunks):
                start = (offset + i) * SUBS * SUBS + c
                field_ref[pl.ds(start, SUBS, stride=SUBS), :] = source[
                    i, :, c * LANES : (c + 1) * LANES
                ]

    def field(col, index):
        start = pl.multiple_of(col * (SUBS * SUBS) + index * SUBS, SUBS)
        return field_ref[pl.ds(start, SUBS), :]

    def shifted(v):
        following = pltpu.roll(v, SUBS - 1, 0)
        shifts = [v] + [
            pltpu.roll(jnp.where(lane < o, following, v), LANES - o, 1) for o in range(1, 4)
        ]
        return [jnp.where(low, z, pltpu.roll(z, HALF, 0)) for z in shifts]

    def value(z, h):
        return sum(table_ref[h, o] * z[o] for o in range(4))

    def slope(d, h):
        return sum(table_ref[h, 4 + o] * d[o] for o in range(3))

    def curve(g, h):
        return table_ref[h, 7] * g[0] + table_ref[h, 8] * g[1]

    def differences(z):
        return [z[o + 1] - z[o] for o in range(len(z) - 1)]

    def axial_take(col, load, carried, thick=None):
        za, zb, zc = (shifted(load(col, i)) for i in range(3))
        da, db, dc = differences(za), differences(zb), differences(zc)
        gc = differences(dc)
        out = []
        for h in range(2):
            old_a0, old_b0, old_c0, old_c1, old_dc0 = carried[h]
            a0, b0, c0, c1 = value(za, h), value(zb, h), value(zc, h), slope(dc, h)
            take_ref[A1, col, h] = slope(da, h)
            take_ref[B1, col, h] = slope(db, h)
            take_ref[C0, col, h] = c0
            take_ref[C1, col, h] = c1
            take_ref[C2, col, h] = curve(gc, h)
            take_ref[DA0, col - 1, h] = a0 - old_a0
            take_ref[DB0, col - 1, h] = b0 - old_b0
            dc0 = c0 - old_c0
            take_ref[DC0, col - 1, h] = dc0
            take_ref[DC1, col - 1, h] = c1 - old_c1
            take_ref[DDC0, col - 2, h] = dc0 - old_dc0
            out.append((a0, b0, c0, c1, dc0))
        if thick is not None:
            zh = shifted(thick(col))
            for h in range(2):
                take_ref[H0, col, h] = value(zh, h)
        return tuple(out)

    nothing = tuple((zero,) * 5 for _ in range(2))

    def takes(name, k, h, taps):
        return [take_ref[name, k + o, h] for o in range(taps)]

    first = pad - HALO
    last = pad + own_cols - 1 + HALO - 3
    lax.fori_loop(
        first,
        last + 4,
        lambda col, carried: axial_take(
            col, field, carried, thick=lambda c: field(c, 6)
        ),
        nothing,
    )
    stringers = []
    for i, source in enumerate((left_ref, own_ref, right_ref)):
        column = jnp.max(source[0, 7:8, 0:LANES]).astype(jnp.int32)
        stringers.append(column + (pad + (i - 1) * own_cols))
    marks = (1.0 / 6.0, 4.0 / 6.0, 1.0 / 6.0)

    def line(name, column, h):
        return sum(marks[j] * take_ref[name, column + j, h] for j in range(3))

    for i, column in enumerate(stringers):
        for h in range(2):
            along, tilt = line(A1, column, h), line(C1, column, h)
            line_ref[i, h, 0] = along + 0.5 * tilt * tilt
            line_ref[i, h, 1] = tilt

    axial_weight = [WEIGHTS[0], WEIGHTS[1]]
    inverse = 1.0 / (1.0 - POISSON * POISSON)

    def prepare(k, unused):
        for h in range(2):
            u1 = take4(takes(A1, k, h, 4))
            us = take3(takes(DA0, k, h, 3))
            vs = take3(takes(DB0, k, h, 3))
            vx = take4(takes(B1, k, h, 4))
            w0 = take4(takes(C0, k, h, 4))
            w1 = take4(takes(C1, k, h, 4))
            ws = take3(takes(DC0, k, h, 3))
            h0 = take4(takes(H0, k, h, 4))
            for p in range(2):
                t = POINTS[p]
                weight = WEIGHTS[p] * axial_weight[h]
                along = both(u1(t))
                across = both(merged(vs(t), w0(t, 1.0 / radius)))
                shear = both(merged(us(t), vx(t)))
                tilt_x, tilt_s, thick = both(w1(t)), both(ws(t)), both(h0(t))
                for q in range(2):
                    wx, wc, th = tilt_x[q], tilt_s[q], thick[q]
                    ex = along[q] + 0.5 * wx * wx
                    es = across[q] + 0.5 * wc * wc
                    g = shear[q] + wx * wc
                    a = th * (inverse * weight)
                    ag = a * (0.5 * (1.0 - POISSON))
                    point = p if q == 0 else 3 - p
                    state_ref[k, h, point, S_WX] = wx
                    state_ref[k, h, point, S_WS] = wc
                    state_ref[k, h, point, S_NX] = a * (ex + POISSON * es)
                    state_ref[k, h, point, S_NS] = a * (POISSON * ex + es)
                    state_ref[k, h, point, S_NG] = ag * g
                    state_ref[k, h, point, S_A] = a
                    state_ref[k, h, point, S_AG] = ag
                    state_ref[k, h, point, S_D] = a * (th * th) * (1.0 / 12.0)
        return unused

    lax.fori_loop(first, last + 1, prepare, 0)

    def add(name, k, h, parts):
        for o, part in enumerate(parts):
            if o == len(parts) - 1:
                acc_ref[name, k + o, h] = part
            else:
                acc_ref[name, k + o, h] += part

    def span(k, unused):
        for h in range(2):
            a1 = take4(takes(A1, k, h, 4))
            b1 = take4(takes(B1, k, h, 4))
            c0 = take4(takes(C0, k, h, 4))
            c1 = take4(takes(C1, k, h, 4))
            c2 = take4(takes(C2, k, h, 4))
            as0 = take3(takes(DA0, k, h, 3))
            bs0 = take3(takes(DB0, k, h, 3))
            cs0 = take3(takes(DC0, k, h, 3))
            cx0 = take3(takes(DC1, k, h, 3))
            cc0 = take2(takes(DDC0, k, h, 2))
            parts = []
            for p in range(2):
                t = POINTS[p]
                along = both(a1(t))
                across = both(merged(bs0(t), c0(t, 1.0 / radius)))
                shear = both(merged(as0(t), b1(t)))
                tilt_x, tilt_s = both(c1(t)), both(cs0(t))
                bend_x, bend_s = both(c2(t)), both(cc0(t))
                twist = both(cx0(t, 2.0 * (1.0 - POISSON)))
                results = []
                for q in range(2):
                    point = p if q == 0 else 3 - p
                    wx, wc = state_ref[k, h, point, S_WX], state_ref[k, h, point, S_WS]
                    cx, cs = tilt_x[q], tilt_s[q]
                    ex = along[q] + wx * cx
                    es = across[q] + wc * cs
                    g = shear[q] + wx * cs + wc * cx
                    a = state_ref[k, h, point, S_A]
                    fx = a * (ex + POISSON * es)
                    fs = a * (POISSON * ex + es)
                    fg = state_ref[k, h, point, S_AG] * g
                    d = state_ref[k, h, point, S_D]
                    mx = d * (bend_x[q] + POISSON * bend_s[q])
                    ms = d * (POISSON * bend_x[q] + bend_s[q])
                    mg = d * twist[q]
                    ng = state_ref[k, h, point, S_NG]
                    sx = fx * wx + fg * wc + state_ref[k, h, point, S_NX] * cx + ng * cs
                    ss = fs * wc + fg * wx + state_ref[k, h, point, S_NS] * cs + ng * cx
                    results.append((fx, fs, fg, mx, ms, mg, sx, ss))
                parts.append((t, list(zip(*results))))

            def pick(i):
                return [(t, values[i]) for t, values in parts]

            add(F01, k, h, put4(pick(0)))
            add(F00, k, h, put3(pick(2)))
            add(F10, k, h, put3(pick(1)))
            add(F11, k, h, put4(pick(2)))
            add(F20, k, h, put4(pick(1), 1.0 / radius))
            add(F20Q, k, h, put3(pick(7)))
            add(F20L, k, h, put2(pick(4)))
            add(F21, k, h, put4(pick(6)))
            add(F21Q, k, h, put3(pick(5)))
            add(F22, k, h, put4(pick(3)))
        return unused

    def back(name, col, h):
        return acc_ref[name, col - 1, h] - acc_ref[name, col, h]

    def axial_put(zeroth, first_, second):
        t = [sum(table_ref[h, o] * zeroth[h] for h in range(2)) for o in range(4)]
        r = [sum(table_ref[h, 4 + o] * first_[h] for h in range(2)) for o in range(3)]
        t = [t[0] - r[0], t[1] + (r[0] - r[1]), t[2] + (r[1] - r[2]), t[3] + r[2]]
        if second is not None:
            l0, l1 = (sum(table_ref[h, 7 + o] * second[h] for h in range(2)) for o in range(2))
            t = [t[0] + l0, t[1] + (l1 - 2.0 * l0), t[2] + (l0 - 2.0 * l1), t[3] + l1]
        stay, cross = t[0], zero
        for o in range(1, 4):
            moved = pltpu.roll(t[o], o, 1)
            stay = stay + jnp.where(lane < o, 0.0, moved)
            cross = cross + jnp.where(lane < o, moved, 0.0)
        stay = jnp.where(low, stay + pltpu.roll(stay, HALF, 0), 0.0)
        cross = jnp.where(low, cross + pltpu.roll(cross, HALF, 0), 0.0)
        return stay + pltpu.roll(cross, 1, 0)

    ends = (sub == 0) | (sub == HALF)

    def end_part(v):
        row = (v + 4.0 * pltpu.roll(v, LANES - 1, 1) + pltpu.roll(v, LANES - 2, 1)) * (
            END_STIFF / 36.0
        )
        row = jnp.where(ends & (lane == 0), row, 0.0)
        return row + 4.0 * pltpu.roll(row, 1, 1) + pltpu.roll(row, 2, 1)

    for step in range(STEPS):
        reach = HALO - 3 * step
        first = pad - reach
        last = pad + own_cols - 1 + reach - 3

        def load(col, index, step=step):
            if step == 0:
                return field(col, 3 + index)
            return image_ref[step - 1, col, index]

        lax.fori_loop(
            first, last + 4, lambda col, carried: axial_take(col, load, carried), nothing
        )
        for name, taps in (
            (F01, 4), (F00, 3), (F10, 3), (F11, 4), (F20, 4),
            (F20Q, 3), (F20L, 2), (F21, 4), (F21Q, 3), (F22, 4),
        ):
            for o in range(taps - 1):
                for h in range(2):
                    acc_ref[name, first + o, h] = zero
        lax.fori_loop(first, last + 1, span, 0)

        for i, column in enumerate(stringers):
            for h in range(2):
                weight = jnp.float32(axial_weight[h])
                stretch, tilt = line_ref[i, h, 0], line_ref[i, h, 1]
                slope_c = line(C1, column, h)
                d_stretch = line(A1, column, h) + tilt * slope_c
                f0 = (STRINGER_AXIAL * weight) * d_stretch
                f1 = (STRINGER_AXIAL * weight) * (d_stretch * tilt + stretch * slope_c)
                f2 = (STRINGER_BENDING * weight) * line(C2, column, h)
                for j in range(3):
                    acc_ref[F01, column + j, h] += marks[j] * f0
                    acc_ref[F21, column + j, h] += marks[j] * f1
                    acc_ref[F22, column + j, h] += marks[j] * f2

        def gather(col, unused, step=step, load=load):
            halves = range(2)
            zeroth = [
                [back(F00, col, h) for h in halves],
                [back(F10, col, h) for h in halves],
                [
                    acc_ref[F20, col, h]
                    + back(F20Q, col, h)
                    + (acc_ref[F20L, col - 2, h] - acc_ref[F20L, col - 1, h])
                    - back(F20L, col, h)
                    for h in halves
                ],
            ]
            first_ = [
                [acc_ref[F01, col, h] for h in halves],
                [acc_ref[F11, col, h] for h in halves],
                [acc_ref[F21, col, h] + back(F21Q, col, h) for h in halves],
            ]
            second = [None, None, [acc_ref[F22, col, h] for h in halves]]
            for i in range(3):
                image_ref[step, col, i] = axial_put(zeroth[i], first_[i], second[i]) + end_part(
                    load(col, i)
                )
            return unused

        lax.fori_loop(first + 3, last + 1, gather, 0)

    pairs = [(i, j) for i in range(STEPS + 1) for j in range(i, STEPS + 1)]

    def inner(i, sums):
        col = pad + i
        sums = list(sums)
        for comp in range(3):
            vectors = [field(col, 3 + comp)] + [image_ref[s, col, comp] for s in range(STEPS)]
            for s, vector in enumerate(vectors):
                start = pl.multiple_of(i * (3 * SUBS) + comp * SUBS, SUBS)
                krylov_ref[s, pl.ds(start, SUBS), :] = vector
            for n, (x, y) in enumerate(pairs):
                sums[n] = sums[n] + vectors[x] * vectors[y]
        return tuple(sums)

    sums = lax.fori_loop(0, own_cols, inner, (zero,) * len(pairs))
    rows = jnp.concatenate(
        [jnp.sum(s, axis=0, keepdims=True) for s in sums]
        + [jnp.zeros((gram_ref.shape[1] - len(pairs), LANES), jnp.float32)],
        axis=0,
    )
    gram_ref[...] = jnp.broadcast_to(rows[None], gram_ref.shape)


def combine_kernel(count_all, gram_ref, krylov_ref, vectors_ref, alpha_ref, beta_ref):
    total = jnp.sum(jnp.sum(gram_ref[...], axis=0), axis=1, keepdims=True) * (1.0 / count_all)
    pairs = [(i, j) for i in range(STEPS + 1) for j in range(i, STEPS + 1)]
    gram = {}
    for n, (i, j) in enumerate(pairs):
        gram[i, j] = gram[j, i] = total[n : n + 1, :]

    def product(x, y):
        return sum(x[i] * (sum(gram[i, j] * y[j] for j in range(len(y)))) for i in range(len(x)))

    def raised(x):
        return [jnp.zeros_like(x[0])] + x

    def less(x, scale, y):
        return [
            x[i] - scale * y[i] if i < len(y) else x[i] for i in range(len(x))
        ]

    current = [jnp.ones_like(total[0:1, :])]
    previous = None
    square = product(current, current) + EPSILON
    scale = square
    alphas, polynomials, scales, betas = [], [], [], []
    for step in range(STEPS):
        image = raised(current)
        alpha = product(current, image) / scale
        following = less(image, alpha, current)
        if previous is not None:
            following = less(following, square, previous)
        previous, current = current, following
        square = product(current, current) / scale + EPSILON
        scale = scale * square
        alphas.append(alpha)
        betas.append(square)
        polynomials.append(current)
        scales.append(scale)
    root = jnp.sqrt(jnp.concatenate(betas, axis=0))
    inverse = [1.0 / jnp.sqrt(s) for s in scales]
    for s in range(STEPS):
        alpha_ref[s] = jnp.max(alphas[s])
        beta_ref[s] = jnp.max(root[s : s + 1, :])
    factors = [
        [jnp.broadcast_to(c * inverse[s], (SUBS, LANES)) for c in polynomials[s]]
        for s in range(STEPS)
    ]
    own_cols, length = vectors_ref.shape[2], vectors_ref.shape[3]
    for comp in range(3):
        for block in range(own_cols // SUBS):
            for c in range((length + LANES - 1) // LANES):
                start = block * SUBS * 3 * SUBS + comp * SUBS + c
                vectors = [
                    krylov_ref[s, pl.ds(start, SUBS, stride=3 * SUBS), :] for s in range(STEPS + 1)
                ]
                width = min(LANES, length - c * LANES)
                for s in range(STEPS):
                    result = sum(factors[s][i] * vectors[i] for i in range(s + 2))
                    vectors_ref[
                        s, comp, block * SUBS : (block + 1) * SUBS, c * LANES : c * LANES + width
                    ] = result[:, :width]


def per_device(state_field, direction, skin_thickness, stringer_column):
    count = lax.axis_size("circ")
    own_cols, axial_count = state_field.shape[1:]
    radius = own_cols * count / (2.0 * math.pi)
    count_all = 3.0 * own_cols * axial_count * count
    pad = own_cols
    padded = -(-axial_count // LANES) * LANES
    columns = 3 * own_cols

    local = (stringer_column - lax.axis_index("circ") * own_cols).astype(jnp.float32)
    packed = jnp.concatenate(
        [
            state_field,
            direction,
            skin_thickness[None],
            jnp.broadcast_to(local[:, None, None], (1, own_cols, axial_count)),
        ],
        axis=0,
    )
    packed = jnp.pad(packed, ((0, 0), (0, 0), (0, padded - axial_count))).transpose(1, 0, 2)
    left = lax.ppermute(
        packed[own_cols - HALO :], "circ", [(i, (i + 1) % count) for i in range(count)]
    )
    right = lax.ppermute(
        packed[:HALO], "circ", [((i + 1) % count, i) for i in range(count)]
    )
    krylov, gram = pl.pallas_call(
        functools.partial(krylov_kernel, own_cols, pad, radius),
        out_shape=(
            jax.ShapeDtypeStruct((STEPS + 1, own_cols * 3 * SUBS, LANES), jnp.float32),
            jax.ShapeDtypeStruct((count, 16, LANES), jnp.float32),
        ),
        in_specs=[pl.BlockSpec(memory_space=pltpu.VMEM)] * 3,
        out_specs=(pl.BlockSpec(memory_space=pltpu.VMEM),) * 2,
        scratch_shapes=[
            pltpu.VMEM((columns * SUBS * SUBS, LANES), jnp.float32),
            pltpu.VMEM((11, columns, 2, SUBS, LANES), jnp.float32),
            pltpu.VMEM((10, columns, 2, SUBS, LANES), jnp.float32),
            pltpu.VMEM((columns, 2, 4, 8, SUBS, LANES), jnp.float32),
            pltpu.VMEM((STEPS, columns, 3, SUBS, LANES), jnp.float32),
            pltpu.VMEM((2, 9, SUBS, LANES), jnp.float32),
            pltpu.VMEM((3, 2, 2, SUBS, LANES), jnp.float32),
        ],
        compiler_params=pltpu.CompilerParams(vmem_limit_bytes=48 * 1024 * 1024),
        name="krylov",
    )(left, packed, right)
    gram = lax.all_to_all(gram, "circ", 0, 0, tiled=True)
    return pl.pallas_call(
        functools.partial(combine_kernel, count_all),
        out_shape=(
            jax.ShapeDtypeStruct((STEPS, 3, own_cols, axial_count), jnp.float32),
            jax.ShapeDtypeStruct((STEPS,), jnp.float32),
            jax.ShapeDtypeStruct((STEPS,), jnp.float32),
        ),
        in_specs=[pl.BlockSpec(memory_space=pltpu.VMEM)] * 2,
        out_specs=(
            pl.BlockSpec(memory_space=pltpu.VMEM),
            pl.BlockSpec(memory_space=pltpu.SMEM),
            pl.BlockSpec(memory_space=pltpu.SMEM),
        ),
        name="combine",
    )(gram, krylov)


def solution(mesh):
    in_specs = (P("group", "circ", None), P("group", "circ", None), P("circ", None), P("circ"))
    out_specs = (P("group", None, "circ", None), P("group"), P("group"))
    return jax.shard_map(
        per_device, mesh=mesh, in_specs=in_specs, out_specs=out_specs, check_vma=False
    )
```

```python
import functools
import math

import jax
import jax.numpy as jnp
from jax import lax
from jax.experimental import pallas as pl
from jax.experimental.pallas import tpu as pltpu
from jax.sharding import PartitionSpec as P

STEPS = 3

POISSON = 0.3
EPSILON = 1e-06
STRINGER_AXIAL = 40.0
STRINGER_BENDING = 20.0
END_STIFF = 4.0

LANES = 128
SUBS = 8
HALF = 4
HALO = 3 * STEPS

A1, B1, C0, C1, C2, DA0, DB0, DC0, DC1, DDC0, H0 = range(11)
F01, F00, F10, F11, F20, F20Q, F20L, F21, F21Q, F22 = range(10)
S_WX, S_WS, S_NX, S_NS, S_NG, S_A, S_AG, S_D = range(8)


def gauss_rule():
    inner_root = math.sqrt(3.0 / 7.0 - 2.0 / 7.0 * math.sqrt(6.0 / 5.0))
    outer_root = math.sqrt(3.0 / 7.0 + 2.0 / 7.0 * math.sqrt(6.0 / 5.0))
    weight_inner = (18.0 + math.sqrt(30.0)) / 72.0
    weight_outer = (18.0 - math.sqrt(30.0)) / 72.0
    points = [
        0.5 - 0.5 * outer_root,
        0.5 - 0.5 * inner_root,
        0.5 + 0.5 * inner_root,
        0.5 + 0.5 * outer_root,
    ]
    return points, [weight_outer, weight_inner, weight_inner, weight_outer]


def cubic(t):
    s = 1.0 - t
    return [
        s**3 / 6.0,
        (3.0 * t**3 - 6.0 * t**2 + 4.0) / 6.0,
        (-3.0 * t**3 + 3.0 * t**2 + 3.0 * t + 1.0) / 6.0,
        t**3 / 6.0,
    ]


def quadratic(t):
    return [(1.0 - t) ** 2 / 2.0, -(t**2) + t + 0.5, t**2 / 2.0]


POINTS, WEIGHTS = gauss_rule()


def take4(z):
    p03, m03, p12, m12 = z[0] + z[3], z[0] - z[3], z[1] + z[2], z[1] - z[2]

    def at(t, scale=1.0):
        b = [scale * x for x in cubic(t)]
        even = p03 * (0.5 * (b[0] + b[3])) + p12 * (0.5 * (b[1] + b[2]))
        odd = m03 * (0.5 * (b[0] - b[3])) + m12 * (0.5 * (b[1] - b[2]))
        return even, odd

    return at


def take3(d):
    p, m = d[0] + d[2], d[0] - d[2]

    def at(t, scale=1.0):
        q = [scale * x for x in quadratic(t)]
        return p * (0.5 * (q[0] + q[2])) + d[1] * q[1], m * (0.5 * (q[0] - q[2]))

    return at


def take2(g):
    even, m = 0.5 * (g[0] + g[1]), g[0] - g[1]

    def at(t):
        return even, m * (0.5 - t)

    return at


def both(pair):
    return pair[0] + pair[1], pair[0] - pair[1]


def merged(first, second):
    return first[0] + second[0], first[1] + second[1]


def put4(pairs, scale=1.0):
    sums = None
    for t, (one, two) in pairs:
        s, d = one + two, one - two
        b = [scale * x for x in cubic(t)]
        terms = [
            s * (0.5 * (b[0] + b[3])),
            d * (0.5 * (b[0] - b[3])),
            s * (0.5 * (b[1] + b[2])),
            d * (0.5 * (b[1] - b[2])),
        ]
        sums = terms if sums is None else [x + y for x, y in zip(sums, terms)]
    e03, o03, e12, o12 = sums
    return [e03 + o03, e12 + o12, e12 - o12, e03 - o03]


def put3(pairs):
    sums = None
    for t, (one, two) in pairs:
        s, d = one + two, one - two
        q = quadratic(t)
        terms = [s * (0.5 * (q[0] + q[2])), d * (0.5 * (q[0] - q[2])), s * q[1]]
        sums = terms if sums is None else [x + y for x, y in zip(sums, terms)]
    even, odd, middle = sums
    return [even + odd, middle, even - odd]


def put2(pairs):
    even, odd = None, None
    for t, (one, two) in pairs:
        s, d = one + two, (one - two) * (0.5 - t)
        even = s if even is None else even + s
        odd = d if odd is None else odd + d
    even = 0.5 * even
    return [even + odd, even - odd]


VECTOR = 11
TAPS = ((F01, 4), (F00, 3), (F10, 3), (F11, 4), (F20, 4), (F20Q, 3), (F20L, 2), (F21, 4), (F21Q, 3), (F22, 4))
PAIRS = [(i, j) for i in range(STEPS + 1) for j in range(i, STEPS + 1)]


def loop(low, high, body, carry, unroll=1):
    rounds = (high - low) // unroll

    def several(i, carry):
        start = low + i * unroll
        return body([start + u for u in range(unroll)], carry)

    if rounds > 0:
        carry = lax.fori_loop(0, rounds, several, carry)
    rest = list(range(low + rounds * unroll, high))
    return body(rest, carry) if rest else carry


def pack_kernel(own_cols, state_ref, direction_ref, thick_ref, column_ref, own_ref, head_ref, tail_ref):
    length = thick_ref.shape[1]
    chunks = own_ref.shape[0] // (own_cols * SUBS)
    local = lax.rem(column_ref[0], own_cols).astype(jnp.float32)

    def put(f, rows, part, c):
        own_ref[pl.ds((c * own_cols + rows) * SUBS + f, SUBS, stride=SUBS), :] = part
        for ref, low in ((head_ref, 0), (tail_ref, own_cols - HALO)):
            start, stop = max(rows, low), min(rows + SUBS, low + HALO)
            if stop - start == SUBS:
                row = (c * HALO + start - low) * SUBS + f
                ref[pl.ds(row, SUBS, stride=SUBS), :] = part
            else:
                for col in range(start, stop):
                    row = (c * HALO + col - low) * SUBS + f
                    ref[row : row + 1, :] = part[col - rows : col - rows + 1]

    sources = [(state_ref.at[i], i) for i in range(3)]
    sources += [(direction_ref.at[i], 3 + i) for i in range(3)] + [(thick_ref, 6)]
    for rows in range(0, own_cols, SUBS):
        for source, f in sources:
            for c in range(chunks):
                width = min(LANES, length - c * LANES)
                part = source[rows : rows + SUBS, c * LANES : c * LANES + width]
                if width < LANES:
                    fill = jnp.zeros((SUBS, LANES - width), jnp.float32)
                    part = jnp.concatenate([part, fill], axis=1)
                put(f, rows, part, c)
        put(7, rows, jnp.full((SUBS, LANES), local), 0)


class Shell:
    def __init__(self, own_cols, pad, radius, field_ref, take_ref, acc_ref, state_ref, table_ref):
        self.own_cols, self.pad, self.radius = own_cols, pad, radius
        self.field_ref, self.take_ref, self.acc_ref = field_ref, take_ref, acc_ref
        self.state_ref, self.table_ref = state_ref, table_ref
        self.sub = lax.broadcasted_iota(jnp.int32, (SUBS, LANES), 0)
        self.lane = lax.broadcasted_iota(jnp.int32, (SUBS, LANES), 1)
        self.low = self.sub < HALF
        self.zero = jnp.zeros((SUBS, LANES), jnp.float32)
        self.nothing = tuple((self.zero,) * 5 for _ in range(2))
        for h in range(2):
            first, second = POINTS[h], POINTS[3 - h]
            rows = (
                list(zip(cubic(first), cubic(second)))
                + list(zip(quadratic(first), quadratic(second)))
                + [(1.0 - first, 1.0 - second), (first, second)]
            )
            for i, (x, y) in enumerate(rows):
                table_ref[h, i] = jnp.where(self.low, jnp.float32(x), jnp.float32(y))

    def spread(self, source, offset, count):
        for c in range(source.shape[0] // (count * SUBS)):
            for i in range(count):
                start = (offset + i) * SUBS * SUBS + c
                row = (c * count + i) * SUBS
                self.field_ref[pl.ds(start, SUBS, stride=SUBS), :] = source[row : row + SUBS, :]

    def field(self, col, index):
        start = col * (SUBS * SUBS) + index * SUBS
        if not isinstance(start, int):
            start = pl.multiple_of(start, SUBS)
        return self.field_ref[pl.ds(start, SUBS), :]

    def shifted(self, v):
        following = pltpu.roll(v, SUBS - 1, 0)
        shifts = [v] + [
            pltpu.roll(jnp.where(self.lane < o, following, v), LANES - o, 1) for o in range(1, 4)
        ]
        return [jnp.where(self.low, z, pltpu.roll(z, HALF, 0)) for z in shifts]

    def value(self, z, h):
        return sum(self.table_ref[h, o] * z[o] for o in range(4))

    def slope(self, d, h):
        return sum(self.table_ref[h, 4 + o] * d[o] for o in range(3))

    def curve(self, g, h):
        return self.table_ref[h, 7] * g[0] + self.table_ref[h, 8] * g[1]

    def axial_take(self, low, high, load, base, carry, thick=False, unroll=2):
        take_ref = self.take_ref

        def differences(z):
            return [z[o + 1] - z[o] for o in range(len(z) - 1)]

        def body(cols, carry):
            loaded = [[load(col, i) for i in range(4 if thick else 3)] for col in cols]
            for col, vectors in zip(cols, loaded):
                za, zb, zc = (self.shifted(v) for v in vectors[:3])
                da, db, dc = differences(za), differences(zb), differences(zc)
                gc = differences(dc)
                zh = self.shifted(vectors[3]) if thick else None
                out = []
                for h in range(2):
                    old_a0, old_b0, old_c0, old_c1, old_dc0 = carry[h]
                    a0, b0, c0 = self.value(za, h), self.value(zb, h), self.value(zc, h)
                    c1, dc0 = self.slope(dc, h), c0 - old_c0
                    take_ref[base + A1, col, h] = self.slope(da, h)
                    take_ref[base + B1, col, h] = self.slope(db, h)
                    take_ref[base + C0, col, h] = c0
                    take_ref[base + C1, col, h] = c1
                    take_ref[base + DA0, col - 1, h] = a0 - old_a0
                    take_ref[base + DB0, col - 1, h] = b0 - old_b0
                    take_ref[base + DC0, col - 1, h] = dc0
                    if thick:
                        take_ref[base + H0, col, h] = self.value(zh, h)
                    else:
                        take_ref[base + C2, col, h] = self.curve(gc, h)
                        take_ref[base + DC1, col - 1, h] = c1 - old_c1
                        take_ref[base + DDC0, col - 2, h] = dc0 - old_dc0
                    out.append((a0, b0, c0, c1, dc0))
                carry = tuple(out)
            return carry

        return loop(low, high, body, carry, unroll)

    def takes(self, name, k, h, taps):
        return [self.take_ref[name, k + o, h] for o in range(taps)]

    def prepare(self, low, high):
        inverse = 1.0 / (1.0 - POISSON * POISSON)
        takes, state_ref = self.takes, self.state_ref

        def body(cols, unused):
            (k,) = cols
            for h in range(2):
                u1 = take4(takes(A1, k, h, 4))
                us = take3(takes(DA0, k, h, 3))
                vs = take3(takes(DB0, k, h, 3))
                vx = take4(takes(B1, k, h, 4))
                w0 = take4(takes(C0, k, h, 4))
                w1 = take4(takes(C1, k, h, 4))
                ws = take3(takes(DC0, k, h, 3))
                h0 = take4(takes(H0, k, h, 4))
                for p in range(2):
                    t = POINTS[p]
                    weight = WEIGHTS[p] * WEIGHTS[h]
                    along = both(u1(t))
                    across = both(merged(vs(t), w0(t, 1.0 / self.radius)))
                    shear = both(merged(us(t), vx(t)))
                    tilt_x, tilt_s, thick = both(w1(t)), both(ws(t)), both(h0(t))
                    for q in range(2):
                        wx, wc, th = tilt_x[q], tilt_s[q], thick[q]
                        ex = along[q] + 0.5 * wx * wx
                        es = across[q] + 0.5 * wc * wc
                        g = shear[q] + wx * wc
                        a = th * (inverse * weight)
                        ag = a * (0.5 * (1.0 - POISSON))
                        point = p if q == 0 else 3 - p
                        state_ref[k, h, point, S_WX] = wx
                        state_ref[k, h, point, S_WS] = wc
                        state_ref[k, h, point, S_NX] = a * (ex + POISSON * es)
                        state_ref[k, h, point, S_NS] = a * (POISSON * ex + es)
                        state_ref[k, h, point, S_NG] = ag * g
                        state_ref[k, h, point, S_A] = a
                        state_ref[k, h, point, S_AG] = ag
                        state_ref[k, h, point, S_D] = a * (th * th) * (1.0 / 12.0)
            return unused

        loop(low, high, body, 0)

    def clear(self, low, count=None):
        for name, taps in TAPS:
            for o in range(taps - 1 if count is None else count):
                for h in range(2):
                    self.acc_ref[name, low + o, h] = self.zero

    def spans(self, low, high, fresh=True):
        takes, state_ref, acc_ref = self.takes, self.state_ref, self.acc_ref

        def add(name, k, h, parts):
            for o, part in enumerate(parts):
                if fresh and o == len(parts) - 1:
                    acc_ref[name, k + o, h] = part
                else:
                    acc_ref[name, k + o, h] += part

        def body(cols, unused):
            (k,) = cols
            for h in range(2):
                a1 = take4(takes(VECTOR + A1, k, h, 4))
                b1 = take4(takes(VECTOR + B1, k, h, 4))
                c0 = take4(takes(VECTOR + C0, k, h, 4))
                c1 = take4(takes(VECTOR + C1, k, h, 4))
                c2 = take4(takes(VECTOR + C2, k, h, 4))
                as0 = take3(takes(VECTOR + DA0, k, h, 3))
                bs0 = take3(takes(VECTOR + DB0, k, h, 3))
                cs0 = take3(takes(VECTOR + DC0, k, h, 3))
                cx0 = take3(takes(VECTOR + DC1, k, h, 3))
                cc0 = take2(takes(VECTOR + DDC0, k, h, 2))
                parts = []
                for p in range(2):
                    t = POINTS[p]
                    along = both(a1(t))
                    across = both(merged(bs0(t), c0(t, 1.0 / self.radius)))
                    shear = both(merged(as0(t), b1(t)))
                    tilt_x, tilt_s = both(c1(t)), both(cs0(t))
                    bend_x, bend_s = both(c2(t)), both(cc0(t))
                    twist = both(cx0(t, 2.0 * (1.0 - POISSON)))
                    results = []
                    for q in range(2):
                        point = p if q == 0 else 3 - p
                        wx, wc = state_ref[k, h, point, S_WX], state_ref[k, h, point, S_WS]
                        cx, cs = tilt_x[q], tilt_s[q]
                        ex = along[q] + wx * cx
                        es = across[q] + wc * cs
                        g = shear[q] + wx * cs + wc * cx
                        a = state_ref[k, h, point, S_A]
                        fx = a * (ex + POISSON * es)
                        fs = a * (POISSON * ex + es)
                        fg = state_ref[k, h, point, S_AG] * g
                        d = state_ref[k, h, point, S_D]
                        mx = d * (bend_x[q] + POISSON * bend_s[q])
                        ms = d * (POISSON * bend_x[q] + bend_s[q])
                        mg = d * twist[q]
                        ng = state_ref[k, h, point, S_NG]
                        sx = fx * wx + fg * wc + state_ref[k, h, point, S_NX] * cx + ng * cs
                        ss = fs * wc + fg * wx + state_ref[k, h, point, S_NS] * cs + ng * cx
                        results.append((fx, fs, fg, mx, ms, mg, sx, ss))
                    parts.append((t, list(zip(*results))))

                def pick(i):
                    return [(t, values[i]) for t, values in parts]

                add(F01, k, h, put4(pick(0)))
                add(F00, k, h, put3(pick(2)))
                add(F10, k, h, put3(pick(1)))
                add(F11, k, h, put4(pick(2)))
                add(F20, k, h, put4(pick(1), 1.0 / self.radius))
                add(F20Q, k, h, put3(pick(7)))
                add(F20L, k, h, put2(pick(4)))
                add(F21, k, h, put4(pick(6)))
                add(F21Q, k, h, put3(pick(5)))
                add(F22, k, h, put4(pick(3)))
            return unused

        loop(low, high, body, 0)

    def axial_put(self, zeroth, first, second):
        table_ref, lane, low = self.table_ref, self.lane, self.low
        t = [sum(table_ref[h, o] * zeroth[h] for h in range(2)) for o in range(4)]
        r = [sum(table_ref[h, 4 + o] * first[h] for h in range(2)) for o in range(3)]
        t = [t[0] - r[0], t[1] + (r[0] - r[1]), t[2] + (r[1] - r[2]), t[3] + r[2]]
        if second is not None:
            l0, l1 = (sum(table_ref[h, 7 + o] * second[h] for h in range(2)) for o in range(2))
            t = [t[0] + l0, t[1] + (l1 - 2.0 * l0), t[2] + (l0 - 2.0 * l1), t[3] + l1]
        stay, cross = t[0], self.zero
        for o in range(1, 4):
            moved = pltpu.roll(t[o], o, 1)
            stay = stay + jnp.where(lane < o, 0.0, moved)
            cross = cross + jnp.where(lane < o, moved, 0.0)
        stay = jnp.where(low, stay + pltpu.roll(stay, HALF, 0), 0.0)
        cross = jnp.where(low, cross + pltpu.roll(cross, HALF, 0), 0.0)
        return stay + pltpu.roll(cross, 1, 0)

    def end_part(self, v):
        corners = ((self.sub == 0) | (self.sub == HALF)) & (self.lane == 0)
        row = (v + 4.0 * pltpu.roll(v, LANES - 1, 1) + pltpu.roll(v, LANES - 2, 1)) * (
            END_STIFF / 36.0
        )
        row = jnp.where(corners, row, 0.0)
        return row + 4.0 * pltpu.roll(row, 1, 1) + pltpu.roll(row, 2, 1)

    def gather(self, low, high, load, image_ref, step, unroll=2):
        acc_ref, halves = self.acc_ref, range(2)

        def back(name, col, h):
            return acc_ref[name, col - 1, h] - acc_ref[name, col, h]

        def body(cols, unused):
            work = []
            for col in cols:
                zeroth = [
                    [back(F00, col, h) for h in halves],
                    [back(F10, col, h) for h in halves],
                    [
                        acc_ref[F20, col, h]
                        + back(F20Q, col, h)
                        + (acc_ref[F20L, col - 2, h] - acc_ref[F20L, col - 1, h])
                        - back(F20L, col, h)
                        for h in halves
                    ],
                ]
                first = [
                    [acc_ref[F01, col, h] for h in halves],
                    [acc_ref[F11, col, h] for h in halves],
                    [acc_ref[F21, col, h] + back(F21Q, col, h) for h in halves],
                ]
                second = [None, None, [acc_ref[F22, col, h] for h in halves]]
                work.append((zeroth, first, second, [load(col, i) for i in range(3)]))
            images = [
                [
                    self.axial_put(zeroth[i], first[i], second[i]) + self.end_part(v[i])
                    for i in range(3)
                ]
                for zeroth, first, second, v in work
            ]
            for col, image in zip(cols, images):
                for i in range(3):
                    image_ref[step, col, i] = image[i]
            return unused

        loop(low, high, body, 0, unroll)


def own_kernel(own_cols, pad, radius, own_ref, field_ref, take_ref, acc_ref, state_ref, carry_ref, table_ref):
    shell = Shell(own_cols, pad, radius, field_ref, take_ref, acc_ref, state_ref, table_ref)
    for col in range(pad, pad + own_cols):
        for i in range(3, 6):
            start = col * SUBS * SUBS + i * SUBS
            field_ref[start : start + SUBS, :] = shell.zero
    shell.spread(own_ref, pad, own_cols)
    stop = pad + own_cols
    carry = shell.axial_take(pad, stop, lambda c, i: shell.field(c, (0, 1, 2, 6)[i]), 0, shell.nothing, thick=True)
    for h in range(2):
        for i in range(5):
            carry_ref[0, h, i] = carry[h][i]
    carry = shell.axial_take(pad, stop, lambda c, i: shell.field(c, 3 + i), VECTOR, shell.nothing)
    for h in range(2):
        for i in range(5):
            carry_ref[1, h, i] = carry[h][i]
    shell.prepare(pad, stop - 3)
    shell.clear(pad)
    shell.spans(pad, stop - 3)


def krylov_kernel(
    own_cols,
    pad,
    radius,
    left_ref,
    right_ref,
    own_ref,
    carry_ref,
    field_in,
    take_in,
    acc_in,
    state_in,
    krylov_ref,
    gram_ref,
    field_ref,
    take_ref,
    acc_ref,
    state_ref,
    image_ref,
    table_ref,
    line_ref,
):
    shell = Shell(own_cols, pad, radius, field_ref, take_ref, acc_ref, state_ref, table_ref)
    field, zero = shell.field, shell.zero
    stop = pad + own_cols
    shell.spread(left_ref, pad - HALO, HALO)
    shell.spread(right_ref, stop, HALO)

    for index, base, names in ((0, 0, (0, 1, 2, 6)), (1, VECTOR, (3, 4, 5))):
        def load(col, i, names=names):
            return field(col, names[i])

        thick = index == 0
        shell.axial_take(pad - HALO, pad + 2, load, base, shell.nothing, thick=thick)
        carry = tuple(tuple(carry_ref[index, h, i] for i in range(5)) for h in range(2))
        shell.axial_take(stop, stop + HALO, load, base, carry, thick=thick)
    shell.prepare(pad - HALO, pad)
    shell.prepare(stop - 3, stop + HALO - 3)

    stringers = []
    for i, source in enumerate((left_ref, own_ref, right_ref)):
        column = jnp.max(source[7:8, :]).astype(jnp.int32)
        stringers.append(column + (pad + (i - 1) * own_cols))
    marks = (1.0 / 6.0, 4.0 / 6.0, 1.0 / 6.0)

    def line(name, column, h):
        return sum(marks[j] * take_ref[name, column + j, h] for j in range(3))

    for i, column in enumerate(stringers):
        for h in range(2):
            along, tilt = line(A1, column, h), line(C1, column, h)
            line_ref[i, h, 0] = along + 0.5 * tilt * tilt
            line_ref[i, h, 1] = tilt

    for step in range(STEPS):
        reach = HALO - 3 * step
        first, last = pad - reach, stop + reach - 3

        def load(col, index, step=step):
            if step == 0:
                return field(col, 3 + index)
            return image_ref[step - 1, col, index]

        if step == 0:
            shell.clear(first, reach)
            shell.spans(first, pad, fresh=False)
            shell.spans(stop - 3, last)
        else:
            shell.axial_take(first, last + 3, load, VECTOR, shell.nothing)
            shell.clear(first)
            shell.spans(first, last)

        for i, column in enumerate(stringers):
            for h in range(2):
                weight = jnp.float32(WEIGHTS[h])
                stretch, tilt = line_ref[i, h, 0], line_ref[i, h, 1]
                slope_c = line(VECTOR + C1, column, h)
                d_stretch = line(VECTOR + A1, column, h) + tilt * slope_c
                f0 = (STRINGER_AXIAL * weight) * d_stretch
                f1 = (STRINGER_AXIAL * weight) * (d_stretch * tilt + stretch * slope_c)
                f2 = (STRINGER_BENDING * weight) * line(VECTOR + C2, column, h)
                for j in range(3):
                    acc_ref[F01, column + j, h] += marks[j] * f0
                    acc_ref[F21, column + j, h] += marks[j] * f1
                    acc_ref[F22, column + j, h] += marks[j] * f2

        shell.gather(first + 3, last, load, image_ref, step)

    def inner(cols, sums):
        sums = list(sums)
        for col in cols:
            for comp in range(3):
                vectors = [field(pad + col, 3 + comp)] + [
                    image_ref[s, pad + col, comp] for s in range(STEPS)
                ]
                for s, vector in enumerate(vectors):
                    start = pl.multiple_of(col * (3 * SUBS) + comp * SUBS, SUBS)
                    krylov_ref[s, pl.ds(start, SUBS), :] = vector
                for n, (x, y) in enumerate(PAIRS):
                    sums[n] = sums[n] + vectors[x] * vectors[y]
        return tuple(sums)

    sums = loop(0, own_cols, inner, (zero,) * len(PAIRS))
    row = jnp.zeros((1, LANES), jnp.float32)
    for n, s in enumerate(sums):
        part = jnp.sum(jnp.sum(s, axis=0, keepdims=True), axis=1, keepdims=True)
        row = jnp.where(shell.lane[0:1] == n, part, row)
    gram_ref[...] = jnp.broadcast_to(row, gram_ref.shape)


def combine_kernel(count_all, gram_ref, krylov_ref, vectors_ref, alpha_ref, beta_ref):
    row = jnp.sum(gram_ref[...], axis=0, keepdims=True) * (1.0 / count_all)
    gram = {}
    for n, (i, j) in enumerate(PAIRS):
        gram[i, j] = gram[j, i] = row[:, n : n + 1]

    def product(x, y):
        return sum(x[i] * (sum(gram[i, j] * y[j] for j in range(len(y)))) for i in range(len(x)))

    def raised(x):
        return [jnp.zeros_like(x[0])] + x

    def less(x, scale, y):
        return [
            x[i] - scale * y[i] if i < len(y) else x[i] for i in range(len(x))
        ]

    current = [jnp.ones((1, 1), jnp.float32)]
    previous = None
    square = product(current, current) + EPSILON
    scale = square
    alphas, polynomials, scales, betas = [], [], [], []
    for step in range(STEPS):
        image = raised(current)
        alpha = product(current, image) / scale
        following = less(image, alpha, current)
        if previous is not None:
            following = less(following, square, previous)
        previous, current = current, following
        square = product(current, current) / scale + EPSILON
        scale = scale * square
        alphas.append(alpha)
        betas.append(square)
        polynomials.append(current)
        scales.append(scale)
    root = jnp.sqrt(jnp.concatenate(betas, axis=0))
    inverse = [1.0 / jnp.sqrt(s) for s in scales]
    for s in range(STEPS):
        alpha_ref[s] = jnp.max(alphas[s])
        beta_ref[s] = jnp.max(root[s : s + 1, :])
    factors = [
        [jnp.broadcast_to(c * inverse[s], (SUBS, LANES)) for c in polynomials[s]]
        for s in range(STEPS)
    ]
    own_cols, length = vectors_ref.shape[2], vectors_ref.shape[3]
    for comp in range(3):
        for block in range(own_cols // SUBS):
            for c in range((length + LANES - 1) // LANES):
                start = block * SUBS * 3 * SUBS + comp * SUBS + c
                vectors = [
                    krylov_ref[s, pl.ds(start, SUBS, stride=3 * SUBS), :] for s in range(STEPS + 1)
                ]
                width = min(LANES, length - c * LANES)
                for s in range(STEPS):
                    result = sum(factors[s][i] * vectors[i] for i in range(s + 2))
                    vectors_ref[
                        s, comp, block * SUBS : (block + 1) * SUBS, c * LANES : c * LANES + width
                    ] = result[:, :width]


def per_device(state_field, direction, skin_thickness, stringer_column):
    count = lax.axis_size("circ")
    own_cols, axial_count = state_field.shape[1:]
    radius = own_cols * count / (2.0 * math.pi)
    count_all = 3.0 * own_cols * axial_count * count
    pad = own_cols
    chunks = -(-axial_count // LANES)
    columns = 3 * own_cols
    vmem = pl.BlockSpec(memory_space=pltpu.VMEM)
    smem = pl.BlockSpec(memory_space=pltpu.SMEM)

    def shape(*dims):
        return jax.ShapeDtypeStruct(dims, jnp.float32)

    def params(mebibytes):
        return pltpu.CompilerParams(vmem_limit_bytes=mebibytes * 1024 * 1024)

    packed, head, tail = pl.pallas_call(
        functools.partial(pack_kernel, own_cols),
        out_shape=(
            shape(chunks * own_cols * SUBS, LANES),
            shape(chunks * HALO * SUBS, LANES),
            shape(chunks * HALO * SUBS, LANES),
        ),
        in_specs=[vmem, vmem, vmem, smem],
        out_specs=(vmem,) * 3,
        compiler_params=params(8),
        name="pack",
    )(state_field, direction, skin_thickness, stringer_column)
    left = lax.ppermute(tail, "circ", [(i, (i + 1) % count) for i in range(count)])
    right = lax.ppermute(head, "circ", [((i + 1) % count, i) for i in range(count)])
    buffers = (
        shape(columns * SUBS * SUBS, LANES),
        shape(21, columns, 2, SUBS, LANES),
        shape(10, columns, 2, SUBS, LANES),
        shape(columns, 2, 4, 8, SUBS, LANES),
    )
    table = pltpu.VMEM((2, 9, SUBS, LANES), jnp.float32)
    *kept, carry = pl.pallas_call(
        functools.partial(own_kernel, own_cols, pad, radius),
        out_shape=buffers + (shape(2, 2, 5, SUBS, LANES),),
        in_specs=[vmem],
        out_specs=(vmem,) * 5,
        scratch_shapes=[table],
        compiler_params=params(4),
        cost_estimate=pl.CostEstimate(flops=40000000, bytes_accessed=20000000, transcendentals=0),
        name="own",
    )(packed)
    krylov, gram, *_ = pl.pallas_call(
        functools.partial(krylov_kernel, own_cols, pad, radius),
        out_shape=(shape(STEPS + 1, own_cols * 3 * SUBS, LANES), shape(count, LANES)) + buffers,
        in_specs=[vmem] * 8,
        out_specs=(vmem,) * 6,
        input_output_aliases={4: 2, 5: 3, 6: 4, 7: 5},
        scratch_shapes=[
            pltpu.VMEM((STEPS, columns, 3, SUBS, LANES), jnp.float32),
            table,
            pltpu.VMEM((3, 2, 2, SUBS, LANES), jnp.float32),
        ],
        compiler_params=params(8),
        name="krylov",
    )(left, right, packed, carry, *kept)
    gram = lax.all_to_all(gram, "circ", 0, 0, tiled=True)
    return pl.pallas_call(
        functools.partial(combine_kernel, count_all),
        out_shape=(shape(STEPS, 3, own_cols, axial_count), shape(STEPS), shape(STEPS)),
        in_specs=[vmem] * 2,
        out_specs=(vmem, smem, smem),
        compiler_params=params(8),
        name="combine",
    )(gram, krylov)


def solution(mesh):
    in_specs = (P("group", "circ", None), P("group", "circ", None), P("circ", None), P("circ"))
    out_specs = (P("group", None, "circ", None), P("group"), P("group"))
    return jax.shard_map(
        per_device, mesh=mesh, in_specs=in_specs, out_specs=out_specs, check_vma=False
    )
```

```python
import functools
import math

import jax
import jax.numpy as jnp
from jax import lax
from jax.experimental import pallas as pl
from jax.experimental.pallas import tpu as pltpu
from jax.sharding import PartitionSpec as P

STEPS = 3

POISSON = 0.3
EPSILON = 1e-06
STRINGER_AXIAL = 40.0
STRINGER_BENDING = 20.0
END_STIFF = 4.0

LANES = 128
SUBS = 8
HALF = 4
HALO = 3 * STEPS

A1, B1, C0, C1, C2, DA0, DB0, DC0, DC1, DDC0, H0 = range(11)
F01, F00, F10, F11, F20, F20Q, F20L, F21, F21Q, F22 = range(10)
S_WX, S_WS, S_NX, S_NS, S_NG, S_A, S_AG, S_D = range(8)


def gauss_rule():
    inner_root = math.sqrt(3.0 / 7.0 - 2.0 / 7.0 * math.sqrt(6.0 / 5.0))
    outer_root = math.sqrt(3.0 / 7.0 + 2.0 / 7.0 * math.sqrt(6.0 / 5.0))
    weight_inner = (18.0 + math.sqrt(30.0)) / 72.0
    weight_outer = (18.0 - math.sqrt(30.0)) / 72.0
    points = [
        0.5 - 0.5 * outer_root,
        0.5 - 0.5 * inner_root,
        0.5 + 0.5 * inner_root,
        0.5 + 0.5 * outer_root,
    ]
    return points, [weight_outer, weight_inner, weight_inner, weight_outer]


def cubic(t):
    s = 1.0 - t
    return [
        s**3 / 6.0,
        (3.0 * t**3 - 6.0 * t**2 + 4.0) / 6.0,
        (-3.0 * t**3 + 3.0 * t**2 + 3.0 * t + 1.0) / 6.0,
        t**3 / 6.0,
    ]


def quadratic(t):
    return [(1.0 - t) ** 2 / 2.0, -(t**2) + t + 0.5, t**2 / 2.0]


POINTS, WEIGHTS = gauss_rule()


def take4(z):
    p03, m03, p12, m12 = z[0] + z[3], z[0] - z[3], z[1] + z[2], z[1] - z[2]
    rest = p03 - p12

    def at(t, scale=1.0):
        b = [scale * x for x in cubic(t)]
        whole = p12 if scale == 1.0 else p12 * scale
        return whole + rest * (b[0] + b[3]), m03 * (b[0] - b[3]) + m12 * (b[1] - b[2])

    return at


def take3(d):
    p, m = d[0] + d[2], d[0] - d[2]

    def at(t, scale=1.0):
        q = [2.0 * scale * x for x in quadratic(t)]
        return p * (0.5 * (q[0] + q[2])) + d[1] * q[1], m * (0.5 * (q[0] - q[2]))

    return at


def take2(g):
    even, m = g[0] + g[1], g[0] - g[1]

    def at(t):
        return even, m * (1.0 - 2.0 * t)

    return at


def both(pair):
    return pair[0] + pair[1], pair[0] - pair[1]


def merged(first, second):
    return first[0] + second[0], first[1] + second[1]


def put4(pairs, scale=1.0):
    total, sums = None, None
    for t, (one, two) in pairs:
        s, d = one + two, one - two
        b = [scale * x for x in cubic(t)]
        total = s if total is None else total + s
        terms = [s * (b[0] + b[3]), d * (b[0] - b[3]), d * (b[1] - b[2])]
        sums = terms if sums is None else [x + y for x, y in zip(sums, terms)]
    e03, o03, o12 = sums
    e12 = (total if scale == 1.0 else total * scale) - e03
    return [e03 + o03, e12 + o12, e12 - o12, e03 - o03]


def put3(pairs):
    sums = None
    for t, (one, two) in pairs:
        s, d = one + two, one - two
        q = [2.0 * x for x in quadratic(t)]
        terms = [s * (0.5 * (q[0] + q[2])), d * (0.5 * (q[0] - q[2])), s * q[1]]
        sums = terms if sums is None else [x + y for x, y in zip(sums, terms)]
    even, odd, middle = sums
    return [even + odd, middle, even - odd]


def put2(pairs):
    even, odd = None, None
    for t, (one, two) in pairs:
        s, d = one + two, (one - two) * (1.0 - 2.0 * t)
        even = s if even is None else even + s
        odd = d if odd is None else odd + d
    return [even + odd, even - odd]


VECTOR = 11
TAPS = ((F01, 4), (F00, 3), (F10, 3), (F11, 4), (F20, 4), (F20Q, 3), (F20L, 2), (F21, 4), (F21Q, 3), (F22, 4))
PAIRS = [(i, j) for i in range(STEPS + 1) for j in range(i, STEPS + 1)]


def loop(low, high, body, carry, unroll=1):
    rounds = (high - low) // unroll

    def several(i, carry):
        start = low + i * unroll
        return body([start + u for u in range(unroll)], carry)

    if rounds > 0:
        carry = lax.fori_loop(0, rounds, several, carry)
    rest = list(range(low + rounds * unroll, high))
    return body(rest, carry) if rest else carry


def pack_kernel(own_cols, fields_ref, column_ref, own_ref, head_ref, tail_ref):
    length = fields_ref.shape[2]
    chunks = own_ref.shape[0] // (own_cols * SUBS)
    local = lax.rem(column_ref[0], own_cols).astype(jnp.float32)

    def put(f, rows, part, c):
        own_ref[pl.ds((c * own_cols + rows) * SUBS + f, SUBS, stride=SUBS), :] = part
        for ref, low in ((head_ref, 0), (tail_ref, own_cols - HALO)):
            start, stop = max(rows, low), min(rows + SUBS, low + HALO)
            if stop - start == SUBS:
                row = (c * HALO + start - low) * SUBS + f
                ref[pl.ds(row, SUBS, stride=SUBS), :] = part
            else:
                for col in range(start, stop):
                    row = (c * HALO + col - low) * SUBS + f
                    ref[row : row + 1, :] = part[col - rows : col - rows + 1]

    for rows in range(0, own_cols, SUBS):
        for f in range(7):
            for c in range(chunks):
                width = min(LANES, length - c * LANES)
                part = fields_ref[f, rows : rows + SUBS, c * LANES : c * LANES + width]
                if width < LANES:
                    fill = jnp.zeros((SUBS, LANES - width), jnp.float32)
                    part = jnp.concatenate([part, fill], axis=1)
                put(f, rows, part, c)
        put(7, rows, jnp.full((SUBS, LANES), local), 0)


class Shell:
    def __init__(self, own_cols, pad, radius, field_ref, take_ref, acc_ref, state_ref, table_ref):
        self.own_cols, self.pad, self.radius = own_cols, pad, radius
        self.field_ref, self.take_ref, self.acc_ref = field_ref, take_ref, acc_ref
        self.state_ref, self.table_ref = state_ref, table_ref
        self.sub = lax.broadcasted_iota(jnp.int32, (SUBS, LANES), 0)
        self.lane = lax.broadcasted_iota(jnp.int32, (SUBS, LANES), 1)
        self.low = self.sub < HALF
        row = jnp.where(self.lane == 1, 4.0, jnp.where(self.lane < 3, 1.0, 0.0))
        self.ends = jnp.where((self.sub == 0) | (self.sub == HALF), row, 0.0)
        self.zero = jnp.zeros((SUBS, LANES), jnp.float32)
        self.nothing = tuple((self.zero,) * 5 for _ in range(2))
        for h in range(2):
            first, second = POINTS[h], POINTS[3 - h]
            rows = (
                list(zip(cubic(first), cubic(second)))
                + list(zip(quadratic(first), quadratic(second)))
                + [(1.0 - first, 1.0 - second), (first, second)]
            )
            for i, (x, y) in enumerate(rows):
                table_ref[h, i] = jnp.where(self.low, jnp.float32(0.5 * x), jnp.float32(0.5 * y))

    def spread(self, source, offset, count):
        for c in range(source.shape[0] // (count * SUBS)):
            for i in range(count):
                start = (offset + i) * SUBS * SUBS + c
                row = (c * count + i) * SUBS
                self.field_ref[pl.ds(start, SUBS, stride=SUBS), :] = source[row : row + SUBS, :]

    def field(self, col, index):
        start = col * (SUBS * SUBS) + index * SUBS
        if not isinstance(start, int):
            start = pl.multiple_of(start, SUBS)
        return self.field_ref[pl.ds(start, SUBS), :]

    def shifted(self, v):
        following = pltpu.roll(v, SUBS - 1, 0)
        shifts = [v] + [
            pltpu.roll(jnp.where(self.lane < o, following, v), LANES - o, 1) for o in range(1, 4)
        ]
        return [jnp.where(self.low, z, pltpu.roll(z, HALF, 0)) for z in shifts]

    def value(self, z, h):
        return sum(self.table_ref[h, o] * z[o] for o in range(4))

    def slope(self, d, h):
        return sum(self.table_ref[h, 4 + o] * d[o] for o in range(3))

    def curve(self, g, h):
        return self.table_ref[h, 7] * g[0] + self.table_ref[h, 8] * g[1]

    def axial_take(self, low, high, load, base, carry, thick=False, unroll=4):
        take_ref = self.take_ref

        def differences(z):
            return [z[o + 1] - z[o] for o in range(len(z) - 1)]

        def body(cols, carry):
            loaded = [[load(col, i) for i in range(4 if thick else 3)] for col in cols]
            for col, vectors in zip(cols, loaded):
                za, zb, zc = (self.shifted(v) for v in vectors[:3])
                da, db, dc = differences(za), differences(zb), differences(zc)
                gc = differences(dc)
                zh = self.shifted(vectors[3]) if thick else None
                out = []
                for h in range(2):
                    old_a0, old_b0, old_c0, old_c1, old_dc0 = carry[h]
                    a0, b0, c0 = self.value(za, h), self.value(zb, h), self.value(zc, h)
                    c1, dc0 = self.slope(dc, h), c0 - old_c0
                    take_ref[base + A1, col, h] = self.slope(da, h)
                    take_ref[base + B1, col, h] = self.slope(db, h)
                    take_ref[base + C0, col, h] = c0
                    take_ref[base + C1, col, h] = c1
                    take_ref[base + DA0, col - 1, h] = a0 - old_a0
                    take_ref[base + DB0, col - 1, h] = b0 - old_b0
                    take_ref[base + DC0, col - 1, h] = dc0
                    if thick:
                        take_ref[base + H0, col, h] = self.value(zh, h)
                    else:
                        take_ref[base + C2, col, h] = self.curve(gc, h)
                        take_ref[base + DC1, col - 1, h] = c1 - old_c1
                        take_ref[base + DDC0, col - 2, h] = dc0 - old_dc0
                    out.append((a0, b0, c0, c1, dc0))
                carry = tuple(out)
            return carry

        return loop(low, high, body, carry, unroll)

    def takes(self, name, k, h, taps):
        return [self.take_ref[name, k + o, h] for o in range(taps)]

    def prepare(self, low, high):
        inverse = 1.0 / (1.0 - POISSON * POISSON)
        takes, state_ref = self.takes, self.state_ref

        def body(cols, unused):
            (k,) = cols
            for h in range(2):
                u1 = take4(takes(A1, k, h, 4))
                us = take3(takes(DA0, k, h, 3))
                vs = take3(takes(DB0, k, h, 3))
                vx = take4(takes(B1, k, h, 4))
                w0 = take4(takes(C0, k, h, 4))
                w1 = take4(takes(C1, k, h, 4))
                ws = take3(takes(DC0, k, h, 3))
                h0 = take4(takes(H0, k, h, 4))
                for p in range(2):
                    t = POINTS[p]
                    weight = WEIGHTS[p] * WEIGHTS[h]
                    along = both(u1(t))
                    across = both(merged(vs(t), w0(t, 1.0 / self.radius)))
                    shear = both(merged(us(t), vx(t)))
                    tilt_x, tilt_s, thick = both(w1(t)), both(ws(t)), both(h0(t))
                    for q in range(2):
                        wx, wc, th = tilt_x[q], tilt_s[q], thick[q]
                        ex = along[q] + 0.5 * wx * wx
                        es = across[q] + 0.5 * wc * wc
                        g = shear[q] + wx * wc
                        a = th * (inverse * weight)
                        ag = a * (0.5 * (1.0 - POISSON))
                        point = p if q == 0 else 3 - p
                        state_ref[k, h, point, S_WX] = wx
                        state_ref[k, h, point, S_WS] = wc
                        state_ref[k, h, point, S_NX] = a * (ex + POISSON * es)
                        state_ref[k, h, point, S_NS] = a * (POISSON * ex + es)
                        state_ref[k, h, point, S_NG] = ag * g
                        state_ref[k, h, point, S_A] = a
                        state_ref[k, h, point, S_AG] = ag
                        state_ref[k, h, point, S_D] = a * (th * th) * (1.0 / 12.0)
            return unused

        loop(low, high, body, 0)

    def clear(self, low, count=None):
        for name, taps in TAPS:
            for o in range(taps - 1 if count is None else count):
                for h in range(2):
                    self.acc_ref[name, low + o, h] = self.zero

    def spans(self, low, high, fresh=True):
        takes, state_ref, acc_ref = self.takes, self.state_ref, self.acc_ref

        def add(name, k, h, parts):
            for o, part in enumerate(parts):
                if fresh and o == len(parts) - 1:
                    acc_ref[name, k + o, h] = part
                else:
                    acc_ref[name, k + o, h] += part

        def body(cols, unused):
            (k,) = cols
            for h in range(2):
                a1 = take4(takes(VECTOR + A1, k, h, 4))
                b1 = take4(takes(VECTOR + B1, k, h, 4))
                c0 = take4(takes(VECTOR + C0, k, h, 4))
                c1 = take4(takes(VECTOR + C1, k, h, 4))
                c2 = take4(takes(VECTOR + C2, k, h, 4))
                as0 = take3(takes(VECTOR + DA0, k, h, 3))
                bs0 = take3(takes(VECTOR + DB0, k, h, 3))
                cs0 = take3(takes(VECTOR + DC0, k, h, 3))
                cx0 = take3(takes(VECTOR + DC1, k, h, 3))
                cc0 = take2(takes(VECTOR + DDC0, k, h, 2))
                parts = []
                for p in range(2):
                    t = POINTS[p]
                    along = both(a1(t))
                    across = both(merged(bs0(t), c0(t, 1.0 / self.radius)))
                    shear = both(merged(as0(t), b1(t)))
                    tilt_x, tilt_s = both(c1(t)), both(cs0(t))
                    bend_x, bend_s = both(c2(t)), both(cc0(t))
                    twist = both(cx0(t, 2.0 * (1.0 - POISSON)))
                    results = []
                    for q in range(2):
                        point = p if q == 0 else 3 - p
                        wx, wc = state_ref[k, h, point, S_WX], state_ref[k, h, point, S_WS]
                        cx, cs = tilt_x[q], tilt_s[q]
                        ex = along[q] + wx * cx
                        es = across[q] + wc * cs
                        g = shear[q] + wx * cs + wc * cx
                        a = state_ref[k, h, point, S_A]
                        fx = a * (ex + POISSON * es)
                        fs = a * (POISSON * ex + es)
                        fg = state_ref[k, h, point, S_AG] * g
                        d = state_ref[k, h, point, S_D]
                        mx = d * (bend_x[q] + POISSON * bend_s[q])
                        ms = d * (POISSON * bend_x[q] + bend_s[q])
                        mg = d * twist[q]
                        ng = state_ref[k, h, point, S_NG]
                        sx = fx * wx + fg * wc + state_ref[k, h, point, S_NX] * cx + ng * cs
                        ss = fs * wc + fg * wx + state_ref[k, h, point, S_NS] * cs + ng * cx
                        results.append((fx, fs, fg, mx, ms, mg, sx, ss))
                    parts.append((t, list(zip(*results))))

                def pick(i):
                    return [(t, values[i]) for t, values in parts]

                add(F01, k, h, put4(pick(0)))
                add(F00, k, h, put3(pick(2)))
                add(F10, k, h, put3(pick(1)))
                add(F11, k, h, put4(pick(2)))
                add(F20, k, h, put4(pick(1), 1.0 / self.radius))
                add(F20Q, k, h, put3(pick(7)))
                add(F20L, k, h, put2(pick(4)))
                add(F21, k, h, put4(pick(6)))
                add(F21Q, k, h, put3(pick(5)))
                add(F22, k, h, put4(pick(3)))
            return unused

        loop(low, high, body, 0)

    def axial_put(self, zeroth, first, second):
        table_ref, lane, low = self.table_ref, self.lane, self.low
        t = [sum(table_ref[h, o] * zeroth[h] for h in range(2)) for o in range(4)]
        r = [sum(table_ref[h, 4 + o] * first[h] for h in range(2)) for o in range(3)]
        t = [t[0] - r[0], t[1] + (r[0] - r[1]), t[2] + (r[1] - r[2]), t[3] + r[2]]
        if second is not None:
            l0, l1 = (sum(table_ref[h, 7 + o] * second[h] for h in range(2)) for o in range(2))
            t = [t[0] + l0, t[1] + (l1 - 2.0 * l0), t[2] + (l0 - 2.0 * l1), t[3] + l1]
        stay, cross = t[0], self.zero
        for o in range(1, 4):
            moved = pltpu.roll(t[o], o, 1)
            stay = stay + jnp.where(lane < o, 0.0, moved)
            cross = cross + jnp.where(lane < o, moved, 0.0)
        stay = jnp.where(low, stay + pltpu.roll(stay, HALF, 0), 0.0)
        cross = jnp.where(low, cross + pltpu.roll(cross, HALF, 0), 0.0)
        return stay + pltpu.roll(cross, 1, 0)

    def end_part(self, v):
        total = jnp.sum(v * self.ends, axis=1, keepdims=True)
        return (total * (END_STIFF / 36.0)) * self.ends

    def gather(self, low, high, load, image_ref, step, unroll=4):
        acc_ref, halves = self.acc_ref, range(2)

        def back(name, col, h):
            return acc_ref[name, col - 1, h] - acc_ref[name, col, h]

        def body(cols, unused):
            work = []
            for col in cols:
                zeroth = [
                    [back(F00, col, h) for h in halves],
                    [back(F10, col, h) for h in halves],
                    [
                        acc_ref[F20, col, h]
                        + back(F20Q, col, h)
                        + (acc_ref[F20L, col - 2, h] - acc_ref[F20L, col - 1, h])
                        - back(F20L, col, h)
                        for h in halves
                    ],
                ]
                first = [
                    [acc_ref[F01, col, h] for h in halves],
                    [acc_ref[F11, col, h] for h in halves],
                    [acc_ref[F21, col, h] + back(F21Q, col, h) for h in halves],
                ]
                second = [None, None, [acc_ref[F22, col, h] for h in halves]]
                work.append((zeroth, first, second, [load(col, i) for i in range(3)]))
            images = [
                [
                    self.axial_put(zeroth[i], first[i], second[i]) + self.end_part(v[i])
                    for i in range(3)
                ]
                for zeroth, first, second, v in work
            ]
            for col, image in zip(cols, images):
                for i in range(3):
                    image_ref[step, col, i] = image[i]
            return unused

        loop(low, high, body, 0, unroll)


def own_kernel(own_cols, pad, radius, own_ref, field_ref, take_ref, acc_ref, state_ref, carry_ref, table_ref):
    shell = Shell(own_cols, pad, radius, field_ref, take_ref, acc_ref, state_ref, table_ref)
    for col in range(pad, pad + own_cols):
        for i in range(3, 6):
            start = col * SUBS * SUBS + i * SUBS
            field_ref[start : start + SUBS, :] = shell.zero
    shell.spread(own_ref, pad, own_cols)
    stop = pad + own_cols
    carry = shell.axial_take(pad, stop, lambda c, i: shell.field(c, (0, 1, 2, 6)[i]), 0, shell.nothing, thick=True)
    for h in range(2):
        for i in range(5):
            carry_ref[0, h, i] = carry[h][i]
    carry = shell.axial_take(pad, stop, lambda c, i: shell.field(c, 3 + i), VECTOR, shell.nothing)
    for h in range(2):
        for i in range(5):
            carry_ref[1, h, i] = carry[h][i]
    shell.prepare(pad, stop - 3)
    shell.clear(pad)
    shell.spans(pad, stop - 3)


def krylov_kernel(
    own_cols,
    pad,
    radius,
    left_ref,
    right_ref,
    own_ref,
    carry_ref,
    field_in,
    take_in,
    acc_in,
    state_in,
    krylov_ref,
    gram_ref,
    field_ref,
    take_ref,
    acc_ref,
    state_ref,
    image_ref,
    table_ref,
    line_ref,
):
    shell = Shell(own_cols, pad, radius, field_ref, take_ref, acc_ref, state_ref, table_ref)
    field, zero = shell.field, shell.zero
    stop = pad + own_cols
    shell.spread(left_ref, pad - HALO, HALO)
    shell.spread(right_ref, stop, HALO)

    for index, base, names in ((0, 0, (0, 1, 2, 6)), (1, VECTOR, (3, 4, 5))):
        def load(col, i, names=names):
            return field(col, names[i])

        thick = index == 0
        shell.axial_take(pad - HALO, pad + 2, load, base, shell.nothing, thick=thick)
        carry = tuple(tuple(carry_ref[index, h, i] for i in range(5)) for h in range(2))
        shell.axial_take(stop, stop + HALO, load, base, carry, thick=thick)
    shell.prepare(pad - HALO, pad)
    shell.prepare(stop - 3, stop + HALO - 3)

    stringers = []
    for i, source in enumerate((left_ref, own_ref, right_ref)):
        column = jnp.max(source[7:8, :]).astype(jnp.int32)
        stringers.append(column + (pad + (i - 1) * own_cols))
    marks = (2.0 / 6.0, 8.0 / 6.0, 2.0 / 6.0)

    def line(name, column, h):
        return sum(marks[j] * take_ref[name, column + j, h] for j in range(3))

    for i, column in enumerate(stringers):
        for h in range(2):
            along, tilt = line(A1, column, h), line(C1, column, h)
            line_ref[i, h, 0] = along + 0.5 * tilt * tilt
            line_ref[i, h, 1] = tilt

    for step in range(STEPS):
        reach = HALO - 3 * step
        first, last = pad - reach, stop + reach - 3

        def load(col, index, step=step):
            if step == 0:
                return field(col, 3 + index)
            return image_ref[step - 1, col, index]

        if step == 0:
            shell.clear(first, reach)
            shell.spans(first, pad, fresh=False)
            shell.spans(stop - 3, last)
        else:
            shell.axial_take(first, last + 3, load, VECTOR, shell.nothing)
            shell.clear(first)
            shell.spans(first, last)

        for i, column in enumerate(stringers):
            for h in range(2):
                weight = jnp.float32(WEIGHTS[h])
                stretch, tilt = line_ref[i, h, 0], line_ref[i, h, 1]
                slope_c = line(VECTOR + C1, column, h)
                d_stretch = line(VECTOR + A1, column, h) + tilt * slope_c
                f0 = (STRINGER_AXIAL * weight) * d_stretch
                f1 = (STRINGER_AXIAL * weight) * (d_stretch * tilt + stretch * slope_c)
                f2 = (STRINGER_BENDING * weight) * line(VECTOR + C2, column, h)
                for j in range(3):
                    acc_ref[F01, column + j, h] += marks[j] * f0
                    acc_ref[F21, column + j, h] += marks[j] * f1
                    acc_ref[F22, column + j, h] += marks[j] * f2

        shell.gather(first + 3, last, load, image_ref, step)

    def inner(cols, sums):
        sums = list(sums)
        for col in cols:
            for comp in range(3):
                vectors = [field(pad + col, 3 + comp)] + [
                    image_ref[s, pad + col, comp] for s in range(STEPS)
                ]
                for s, vector in enumerate(vectors):
                    start = pl.multiple_of(col * (3 * SUBS) + comp * SUBS, SUBS)
                    krylov_ref[s, pl.ds(start, SUBS), :] = vector
                for n, (x, y) in enumerate(PAIRS):
                    sums[n] = sums[n] + vectors[x] * vectors[y]
        return tuple(sums)

    sums = loop(0, own_cols, inner, (zero,) * len(PAIRS), 4)
    row = jnp.zeros((1, LANES), jnp.float32)
    for n, s in enumerate(sums):
        part = jnp.sum(jnp.sum(s, axis=0, keepdims=True), axis=1, keepdims=True)
        row = jnp.where(shell.lane[0:1] == n, part, row)
    gram_ref[...] = jnp.broadcast_to(row, gram_ref.shape)


def combine_kernel(count_all, gram_ref, krylov_ref, vectors_ref, alpha_ref, beta_ref):
    row = jnp.sum(gram_ref[...], axis=0, keepdims=True) * (1.0 / count_all)
    gram = {}
    for n, (i, j) in enumerate(PAIRS):
        gram[i, j] = gram[j, i] = row[:, n : n + 1]

    def product(x, y):
        return sum(x[i] * (sum(gram[i, j] * y[j] for j in range(len(y)))) for i in range(len(x)))

    def raised(x):
        return [jnp.zeros_like(x[0])] + x

    def less(x, scale, y):
        return [
            x[i] - scale * y[i] if i < len(y) else x[i] for i in range(len(x))
        ]

    current = [jnp.ones((1, 1), jnp.float32)]
    previous = None
    square = product(current, current) + EPSILON
    scale = square
    alphas, polynomials, scales, betas = [], [], [], []
    for step in range(STEPS):
        image = raised(current)
        alpha = product(current, image) / scale
        following = less(image, alpha, current)
        if previous is not None:
            following = less(following, square, previous)
        previous, current = current, following
        square = product(current, current) / scale + EPSILON
        scale = scale * square
        alphas.append(alpha)
        betas.append(square)
        polynomials.append(current)
        scales.append(scale)
    root = jnp.sqrt(jnp.concatenate(betas, axis=0))
    inverse = [1.0 / jnp.sqrt(s) for s in scales]
    for s in range(STEPS):
        alpha_ref[s] = jnp.max(alphas[s])
        beta_ref[s] = jnp.max(root[s : s + 1, :])
    factors = [
        [jnp.broadcast_to(c * inverse[s], (SUBS, LANES)) for c in polynomials[s]]
        for s in range(STEPS)
    ]
    own_cols, length = vectors_ref.shape[2], vectors_ref.shape[3]
    for comp in range(3):
        for block in range(own_cols // SUBS):
            for c in range((length + LANES - 1) // LANES):
                start = block * SUBS * 3 * SUBS + comp * SUBS + c
                vectors = [
                    krylov_ref[s, pl.ds(start, SUBS, stride=3 * SUBS), :] for s in range(STEPS + 1)
                ]
                width = min(LANES, length - c * LANES)
                for s in range(STEPS):
                    result = sum(factors[s][i] * vectors[i] for i in range(s + 2))
                    vectors_ref[
                        s, comp, block * SUBS : (block + 1) * SUBS, c * LANES : c * LANES + width
                    ] = result[:, :width]


def per_device(state_field, direction, skin_thickness, stringer_column):
    count = lax.axis_size("circ")
    own_cols, axial_count = state_field.shape[1:]
    radius = own_cols * count / (2.0 * math.pi)
    count_all = 3.0 * own_cols * axial_count * count
    pad = own_cols
    chunks = -(-axial_count // LANES)
    columns = 3 * own_cols
    vmem = pl.BlockSpec(memory_space=pltpu.VMEM)
    smem = pl.BlockSpec(memory_space=pltpu.SMEM)

    def shape(*dims):
        return jax.ShapeDtypeStruct(dims, jnp.float32)

    def params(mebibytes):
        return pltpu.CompilerParams(vmem_limit_bytes=mebibytes * 1024 * 1024)

    fields = jnp.concatenate([state_field, direction, skin_thickness[None]], axis=0)
    packed, head, tail = pl.pallas_call(
        functools.partial(pack_kernel, own_cols),
        out_shape=(
            shape(chunks * own_cols * SUBS, LANES),
            shape(chunks * HALO * SUBS, LANES),
            shape(chunks * HALO * SUBS, LANES),
        ),
        in_specs=[vmem, smem],
        out_specs=(vmem,) * 3,
        compiler_params=params(8),
        name="pack",
    )(fields, stringer_column)
    left = lax.ppermute(tail, "circ", [(i, (i + 1) % count) for i in range(count)])
    right = lax.ppermute(head, "circ", [((i + 1) % count, i) for i in range(count)])
    buffers = (
        shape(columns * SUBS * SUBS, LANES),
        shape(21, columns, 2, SUBS, LANES),
        shape(10, columns, 2, SUBS, LANES),
        shape(columns, 2, 4, 8, SUBS, LANES),
    )
    table = pltpu.VMEM((2, 9, SUBS, LANES), jnp.float32)
    *kept, carry = pl.pallas_call(
        functools.partial(own_kernel, own_cols, pad, radius),
        out_shape=buffers + (shape(2, 2, 5, SUBS, LANES),),
        in_specs=[vmem],
        out_specs=(vmem,) * 5,
        scratch_shapes=[table],
        compiler_params=params(4),
        cost_estimate=pl.CostEstimate(flops=40000000, bytes_accessed=20000000, transcendentals=0),
        name="own",
    )(packed)
    krylov, gram, *_ = pl.pallas_call(
        functools.partial(krylov_kernel, own_cols, pad, radius),
        out_shape=(shape(STEPS + 1, own_cols * 3 * SUBS, LANES), shape(count, LANES)) + buffers,
        in_specs=[vmem] * 8,
        out_specs=(vmem,) * 6,
        input_output_aliases={4: 2, 5: 3, 6: 4, 7: 5},
        scratch_shapes=[
            pltpu.VMEM((STEPS, columns, 3, SUBS, LANES), jnp.float32),
            table,
            pltpu.VMEM((3, 2, 2, SUBS, LANES), jnp.float32),
        ],
        compiler_params=params(8),
        name="krylov",
    )(left, right, packed, carry, *kept)
    gram = lax.all_to_all(gram, "circ", 0, 0, tiled=True)
    return pl.pallas_call(
        functools.partial(combine_kernel, count_all),
        out_shape=(shape(STEPS, 3, own_cols, axial_count), shape(STEPS), shape(STEPS)),
        in_specs=[vmem] * 2,
        out_specs=(vmem, smem, smem),
        compiler_params=params(8),
        name="combine",
    )(gram, krylov)


def solution(mesh):
    in_specs = (P("group", "circ", None), P("group", "circ", None), P("circ", None), P("circ"))
    out_specs = (P("group", None, "circ", None), P("group"), P("group"))
    return jax.shard_map(
        per_device, mesh=mesh, in_specs=in_specs, out_specs=out_specs, check_vma=False
    )
```

```python
import functools
import math

import jax
import jax.numpy as jnp
from jax import lax
from jax.experimental import pallas as pl
from jax.experimental.pallas import tpu as pltpu
from jax.sharding import PartitionSpec as P

STEPS = 3

POISSON = 0.3
EPSILON = 1e-06
STRINGER_AXIAL = 40.0
STRINGER_BENDING = 20.0
END_STIFF = 4.0

LANES = 128
SUBS = 8
HALF = 4
HALO = 3 * STEPS

A1, B1, C0, C1, C2, DA0, DB0, DC0, DC1, DDC0, H0 = range(11)
F01, F00, F10, F11, F20, F20Q, F20L, F21, F21Q, F22 = range(10)
S_WX, S_WS, S_NX, S_NS, S_NG, S_A, S_AG, S_D = range(8)


def gauss_rule():
    inner_root = math.sqrt(3.0 / 7.0 - 2.0 / 7.0 * math.sqrt(6.0 / 5.0))
    outer_root = math.sqrt(3.0 / 7.0 + 2.0 / 7.0 * math.sqrt(6.0 / 5.0))
    weight_inner = (18.0 + math.sqrt(30.0)) / 72.0
    weight_outer = (18.0 - math.sqrt(30.0)) / 72.0
    points = [
        0.5 - 0.5 * outer_root,
        0.5 - 0.5 * inner_root,
        0.5 + 0.5 * inner_root,
        0.5 + 0.5 * outer_root,
    ]
    return points, [weight_outer, weight_inner, weight_inner, weight_outer]


def cubic(t):
    s = 1.0 - t
    return [
        s**3 / 6.0,
        (3.0 * t**3 - 6.0 * t**2 + 4.0) / 6.0,
        (-3.0 * t**3 + 3.0 * t**2 + 3.0 * t + 1.0) / 6.0,
        t**3 / 6.0,
    ]


def quadratic(t):
    return [(1.0 - t) ** 2 / 2.0, -(t**2) + t + 0.5, t**2 / 2.0]


POINTS, WEIGHTS = gauss_rule()


def take4(z):
    p03, m03, p12, m12 = z[0] + z[3], z[0] - z[3], z[1] + z[2], z[1] - z[2]
    rest = p03 - p12

    def at(t, scale=1.0):
        b = [scale * x for x in cubic(t)]
        whole = p12 if scale == 1.0 else p12 * scale
        return whole + rest * (b[0] + b[3]), m03 * (b[0] - b[3]) + m12 * (b[1] - b[2])

    return at


def take3(d):
    p, m = d[0] + d[2], d[0] - d[2]

    def at(t, scale=1.0):
        q = [2.0 * scale * x for x in quadratic(t)]
        return p * (0.5 * (q[0] + q[2])) + d[1] * q[1], m * (0.5 * (q[0] - q[2]))

    return at


def take2(g):
    even, m = g[0] + g[1], g[0] - g[1]

    def at(t):
        return even, m * (1.0 - 2.0 * t)

    return at


def both(pair):
    return pair[0] + pair[1], pair[0] - pair[1]


def merged(first, second):
    return first[0] + second[0], first[1] + second[1]


def put4(pairs, scale=1.0):
    total, sums = None, None
    for t, (one, two) in pairs:
        s, d = one + two, one - two
        b = [scale * x for x in cubic(t)]
        total = s if total is None else total + s
        terms = [s * (b[0] + b[3]), d * (b[0] - b[3]), d * (b[1] - b[2])]
        sums = terms if sums is None else [x + y for x, y in zip(sums, terms)]
    e03, o03, o12 = sums
    e12 = (total if scale == 1.0 else total * scale) - e03
    return [e03 + o03, e12 + o12, e12 - o12, e03 - o03]


def put3(pairs):
    sums = None
    for t, (one, two) in pairs:
        s, d = one + two, one - two
        q = [2.0 * x for x in quadratic(t)]
        terms = [s * (0.5 * (q[0] + q[2])), d * (0.5 * (q[0] - q[2])), s * q[1]]
        sums = terms if sums is None else [x + y for x, y in zip(sums, terms)]
    even, odd, middle = sums
    return [even + odd, middle, even - odd]


def put2(pairs):
    even, odd = None, None
    for t, (one, two) in pairs:
        s, d = one + two, (one - two) * (1.0 - 2.0 * t)
        even = s if even is None else even + s
        odd = d if odd is None else odd + d
    return [even + odd, even - odd]


VECTOR = 11
MARKS = (2.0 / 6.0, 8.0 / 6.0, 2.0 / 6.0)
TAPS = ((F01, 4), (F00, 3), (F10, 3), (F11, 4), (F20, 4), (F20Q, 3), (F20L, 2), (F21, 4), (F21Q, 3), (F22, 4))
PAIRS = [(i, j) for i in range(STEPS + 1) for j in range(i, STEPS + 1)]


def loop(low, high, body, carry, unroll=1):
    rounds = (high - low) // unroll

    def several(i, carry):
        start = low + i * unroll
        return body([start + u for u in range(unroll)], carry)

    if rounds > 0:
        carry = lax.fori_loop(0, rounds, several, carry)
    rest = list(range(low + rounds * unroll, high))
    return body(rest, carry) if rest else carry


def pack_kernel(own_cols, fields_ref, column_ref, own_ref, head_ref, tail_ref):
    length = fields_ref.shape[2]
    chunks = own_ref.shape[0] // (own_cols * SUBS)
    local = lax.rem(column_ref[0], own_cols).astype(jnp.float32)

    def put(f, rows, part, c):
        own_ref[pl.ds((c * own_cols + rows) * SUBS + f, SUBS, stride=SUBS), :] = part
        for ref, low in ((head_ref, 0), (tail_ref, own_cols - HALO)):
            start, stop = max(rows, low), min(rows + SUBS, low + HALO)
            if stop - start == SUBS:
                row = (c * HALO + start - low) * SUBS + f
                ref[pl.ds(row, SUBS, stride=SUBS), :] = part
            else:
                for col in range(start, stop):
                    row = (c * HALO + col - low) * SUBS + f
                    ref[row : row + 1, :] = part[col - rows : col - rows + 1]

    for rows in range(0, own_cols, SUBS):
        for f in range(7):
            for c in range(chunks):
                width = min(LANES, length - c * LANES)
                part = fields_ref[f, rows : rows + SUBS, c * LANES : c * LANES + width]
                if width < LANES:
                    fill = jnp.zeros((SUBS, LANES - width), jnp.float32)
                    part = jnp.concatenate([part, fill], axis=1)
                put(f, rows, part, c)
        put(7, rows, jnp.full((SUBS, LANES), local), 0)


class Shell:
    def __init__(self, own_cols, pad, radius, field_ref, take_ref, acc_ref, state_ref, table_ref):
        self.own_cols, self.pad, self.radius = own_cols, pad, radius
        self.field_ref, self.take_ref, self.acc_ref = field_ref, take_ref, acc_ref
        self.state_ref, self.table_ref = state_ref, table_ref
        self.sub = lax.broadcasted_iota(jnp.int32, (SUBS, LANES), 0)
        self.lane = lax.broadcasted_iota(jnp.int32, (SUBS, LANES), 1)
        self.low = self.sub < HALF
        row = jnp.where(self.lane == 1, 4.0, jnp.where(self.lane < 3, 1.0, 0.0))
        self.ends = jnp.where((self.sub == 0) | (self.sub == HALF), row, 0.0)
        self.zero = jnp.zeros((SUBS, LANES), jnp.float32)
        self.nothing = tuple((self.zero,) * 5 for _ in range(2))
        for h in range(2):
            first, second = POINTS[h], POINTS[3 - h]
            rows = (
                list(zip(cubic(first), cubic(second)))
                + list(zip(quadratic(first), quadratic(second)))
                + [(1.0 - first, 1.0 - second), (first, second)]
            )
            for i, (x, y) in enumerate(rows):
                table_ref[h, i] = jnp.where(self.low, jnp.float32(0.5 * x), jnp.float32(0.5 * y))

    def spread(self, source, offset, count):
        for c in range(source.shape[0] // (count * SUBS)):
            for i in range(count):
                start = (offset + i) * SUBS * SUBS + c
                row = (c * count + i) * SUBS
                self.field_ref[pl.ds(start, SUBS, stride=SUBS), :] = source[row : row + SUBS, :]

    def field(self, col, index):
        start = col * (SUBS * SUBS) + index * SUBS
        if not isinstance(start, int):
            start = pl.multiple_of(start, SUBS)
        return self.field_ref[pl.ds(start, SUBS), :]

    def shifted(self, v):
        following = pltpu.roll(v, SUBS - 1, 0)
        shifts = [v] + [
            pltpu.roll(jnp.where(self.lane < o, following, v), LANES - o, 1) for o in range(1, 4)
        ]
        return [jnp.where(self.low, z, pltpu.roll(z, HALF, 0)) for z in shifts]

    def value(self, z, h):
        return sum(self.table_ref[h, o] * z[o] for o in range(4))

    def slope(self, d, h):
        return sum(self.table_ref[h, 4 + o] * d[o] for o in range(3))

    def curve(self, g, h):
        return self.table_ref[h, 7] * g[0] + self.table_ref[h, 8] * g[1]

    def axial_take(self, low, high, load, base, carry, thick=False, unroll=4):
        take_ref = self.take_ref

        def differences(z):
            return [z[o + 1] - z[o] for o in range(len(z) - 1)]

        def body(cols, carry):
            loaded = [[load(col, i) for i in range(4 if thick else 3)] for col in cols]
            for col, vectors in zip(cols, loaded):
                za, zb, zc = (self.shifted(v) for v in vectors[:3])
                da, db, dc = differences(za), differences(zb), differences(zc)
                gc = differences(dc)
                zh = self.shifted(vectors[3]) if thick else None
                out = []
                for h in range(2):
                    old_a0, old_b0, old_c0, old_c1, old_dc0 = carry[h]
                    a0, b0, c0 = self.value(za, h), self.value(zb, h), self.value(zc, h)
                    c1, dc0 = self.slope(dc, h), c0 - old_c0
                    take_ref[base + A1, col, h] = self.slope(da, h)
                    take_ref[base + B1, col, h] = self.slope(db, h)
                    take_ref[base + C0, col, h] = c0
                    take_ref[base + C1, col, h] = c1
                    take_ref[base + DA0, col - 1, h] = a0 - old_a0
                    take_ref[base + DB0, col - 1, h] = b0 - old_b0
                    take_ref[base + DC0, col - 1, h] = dc0
                    if thick:
                        take_ref[base + H0, col, h] = self.value(zh, h)
                    else:
                        take_ref[base + C2, col, h] = self.curve(gc, h)
                        take_ref[base + DC1, col - 1, h] = c1 - old_c1
                        take_ref[base + DDC0, col - 2, h] = dc0 - old_dc0
                    out.append((a0, b0, c0, c1, dc0))
                carry = tuple(out)
            return carry

        return loop(low, high, body, carry, unroll)

    def takes(self, name, k, h, taps):
        return [self.take_ref[name, k + o, h] for o in range(taps)]

    def prepare(self, low, high):
        inverse = 1.0 / (1.0 - POISSON * POISSON)
        takes, state_ref = self.takes, self.state_ref

        def body(cols, unused):
            (k,) = cols
            for h in range(2):
                u1 = take4(takes(A1, k, h, 4))
                us = take3(takes(DA0, k, h, 3))
                vs = take3(takes(DB0, k, h, 3))
                vx = take4(takes(B1, k, h, 4))
                w0 = take4(takes(C0, k, h, 4))
                w1 = take4(takes(C1, k, h, 4))
                ws = take3(takes(DC0, k, h, 3))
                h0 = take4(takes(H0, k, h, 4))
                for p in range(2):
                    t = POINTS[p]
                    weight = WEIGHTS[p] * WEIGHTS[h]
                    along = both(u1(t))
                    across = both(merged(vs(t), w0(t, 1.0 / self.radius)))
                    shear = both(merged(us(t), vx(t)))
                    tilt_x, tilt_s, thick = both(w1(t)), both(ws(t)), both(h0(t))
                    for q in range(2):
                        wx, wc, th = tilt_x[q], tilt_s[q], thick[q]
                        ex = along[q] + 0.5 * wx * wx
                        es = across[q] + 0.5 * wc * wc
                        g = shear[q] + wx * wc
                        a = th * (inverse * weight)
                        ag = a * (0.5 * (1.0 - POISSON))
                        point = p if q == 0 else 3 - p
                        state_ref[k, h, point, S_WX] = wx
                        state_ref[k, h, point, S_WS] = wc
                        state_ref[k, h, point, S_NX] = a * (ex + POISSON * es)
                        state_ref[k, h, point, S_NS] = a * (POISSON * ex + es)
                        state_ref[k, h, point, S_NG] = ag * g
                        state_ref[k, h, point, S_A] = a
                        state_ref[k, h, point, S_AG] = ag
                        state_ref[k, h, point, S_D] = a * (th * th) * (1.0 / 12.0)
            return unused

        loop(low, high, body, 0)

    def clear(self, low, count=None):
        for name, taps in TAPS:
            for o in range(taps - 1 if count is None else count):
                for h in range(2):
                    self.acc_ref[name, low + o, h] = self.zero

    def spans(self, low, high, fresh=True):
        takes, state_ref, acc_ref = self.takes, self.state_ref, self.acc_ref

        def add(name, k, h, parts):
            for o, part in enumerate(parts):
                if fresh and o == len(parts) - 1:
                    acc_ref[name, k + o, h] = part
                else:
                    acc_ref[name, k + o, h] += part

        def body(cols, unused):
            (k,) = cols
            for h in range(2):
                a1 = take4(takes(VECTOR + A1, k, h, 4))
                b1 = take4(takes(VECTOR + B1, k, h, 4))
                c0 = take4(takes(VECTOR + C0, k, h, 4))
                c1 = take4(takes(VECTOR + C1, k, h, 4))
                c2 = take4(takes(VECTOR + C2, k, h, 4))
                as0 = take3(takes(VECTOR + DA0, k, h, 3))
                bs0 = take3(takes(VECTOR + DB0, k, h, 3))
                cs0 = take3(takes(VECTOR + DC0, k, h, 3))
                cx0 = take3(takes(VECTOR + DC1, k, h, 3))
                cc0 = take2(takes(VECTOR + DDC0, k, h, 2))
                parts = []
                for p in range(2):
                    t = POINTS[p]
                    along = both(a1(t))
                    across = both(merged(bs0(t), c0(t, 1.0 / self.radius)))
                    shear = both(merged(as0(t), b1(t)))
                    tilt_x, tilt_s = both(c1(t)), both(cs0(t))
                    bend_x, bend_s = both(c2(t)), both(cc0(t))
                    twist = both(cx0(t, 2.0 * (1.0 - POISSON)))
                    results = []
                    for q in range(2):
                        point = p if q == 0 else 3 - p
                        wx, wc = state_ref[k, h, point, S_WX], state_ref[k, h, point, S_WS]
                        cx, cs = tilt_x[q], tilt_s[q]
                        ex = along[q] + wx * cx
                        es = across[q] + wc * cs
                        g = shear[q] + wx * cs + wc * cx
                        a = state_ref[k, h, point, S_A]
                        fx = a * (ex + POISSON * es)
                        fs = a * (POISSON * ex + es)
                        fg = state_ref[k, h, point, S_AG] * g
                        d = state_ref[k, h, point, S_D]
                        mx = d * (bend_x[q] + POISSON * bend_s[q])
                        ms = d * (POISSON * bend_x[q] + bend_s[q])
                        mg = d * twist[q]
                        ng = state_ref[k, h, point, S_NG]
                        sx = fx * wx + fg * wc + state_ref[k, h, point, S_NX] * cx + ng * cs
                        ss = fs * wc + fg * wx + state_ref[k, h, point, S_NS] * cs + ng * cx
                        results.append((fx, fs, fg, mx, ms, mg, sx, ss))
                    parts.append((t, list(zip(*results))))

                def pick(i):
                    return [(t, values[i]) for t, values in parts]

                add(F01, k, h, put4(pick(0)))
                add(F00, k, h, put3(pick(2)))
                add(F10, k, h, put3(pick(1)))
                add(F11, k, h, put4(pick(2)))
                add(F20, k, h, put4(pick(1), 1.0 / self.radius))
                add(F20Q, k, h, put3(pick(7)))
                add(F20L, k, h, put2(pick(4)))
                add(F21, k, h, put4(pick(6)))
                add(F21Q, k, h, put3(pick(5)))
                add(F22, k, h, put4(pick(3)))
            return unused

        loop(low, high, body, 0)

    def axial_put(self, zeroth, first, second):
        table_ref, lane, low = self.table_ref, self.lane, self.low
        t = [sum(table_ref[h, o] * zeroth[h] for h in range(2)) for o in range(4)]
        r = [sum(table_ref[h, 4 + o] * first[h] for h in range(2)) for o in range(3)]
        t = [t[0] - r[0], t[1] + (r[0] - r[1]), t[2] + (r[1] - r[2]), t[3] + r[2]]
        if second is not None:
            l0, l1 = (sum(table_ref[h, 7 + o] * second[h] for h in range(2)) for o in range(2))
            t = [t[0] + l0, t[1] + (l1 - 2.0 * l0), t[2] + (l0 - 2.0 * l1), t[3] + l1]
        stay, cross = t[0], self.zero
        for o in range(1, 4):
            moved = pltpu.roll(t[o], o, 1)
            stay = stay + jnp.where(lane < o, 0.0, moved)
            cross = cross + jnp.where(lane < o, moved, 0.0)
        stay = jnp.where(low, stay + pltpu.roll(stay, HALF, 0), 0.0)
        cross = jnp.where(low, cross + pltpu.roll(cross, HALF, 0), 0.0)
        return stay + pltpu.roll(cross, 1, 0)

    def end_part(self, v):
        total = jnp.sum(v * self.ends, axis=1, keepdims=True)
        return (total * (END_STIFF / 36.0)) * self.ends

    def line(self, name, column, h):
        return sum(MARKS[j] * self.take_ref[name, column + j, h] for j in range(3))

    def line_state(self, column, h):
        along, tilt = self.line(A1, column, h), self.line(C1, column, h)
        return along + 0.5 * tilt * tilt, tilt

    def stringer(self, column, states):
        for h in range(2):
            weight = jnp.float32(WEIGHTS[h])
            stretch, tilt = states[h]
            slope_c = self.line(VECTOR + C1, column, h)
            d_stretch = self.line(VECTOR + A1, column, h) + tilt * slope_c
            f0 = (STRINGER_AXIAL * weight) * d_stretch
            f1 = (STRINGER_AXIAL * weight) * (d_stretch * tilt + stretch * slope_c)
            f2 = (STRINGER_BENDING * weight) * self.line(VECTOR + C2, column, h)
            for j in range(3):
                self.acc_ref[F01, column + j, h] += MARKS[j] * f0
                self.acc_ref[F21, column + j, h] += MARKS[j] * f1
                self.acc_ref[F22, column + j, h] += MARKS[j] * f2

    def gather(self, low, high, load, image_ref, step, unroll=4):
        acc_ref, halves = self.acc_ref, range(2)

        def back(name, col, h):
            return acc_ref[name, col - 1, h] - acc_ref[name, col, h]

        def body(cols, unused):
            work = []
            for col in cols:
                zeroth = [
                    [back(F00, col, h) for h in halves],
                    [back(F10, col, h) for h in halves],
                    [
                        acc_ref[F20, col, h]
                        + back(F20Q, col, h)
                        + (acc_ref[F20L, col - 2, h] - acc_ref[F20L, col - 1, h])
                        - back(F20L, col, h)
                        for h in halves
                    ],
                ]
                first = [
                    [acc_ref[F01, col, h] for h in halves],
                    [acc_ref[F11, col, h] for h in halves],
                    [acc_ref[F21, col, h] + back(F21Q, col, h) for h in halves],
                ]
                second = [None, None, [acc_ref[F22, col, h] for h in halves]]
                work.append((zeroth, first, second, [load(col, i) for i in range(3)]))
            images = [
                [
                    self.axial_put(zeroth[i], first[i], second[i]) + self.end_part(v[i])
                    for i in range(3)
                ]
                for zeroth, first, second, v in work
            ]
            for col, image in zip(cols, images):
                for i in range(3):
                    image_ref[step, col, i] = image[i]
            return unused

        loop(low, high, body, 0, unroll)


def attached(source, shift):
    return jnp.max(source[7:8, :]).astype(jnp.int32) + shift


def keep(ref, index, carry):
    for h in range(2):
        for i in range(5):
            ref[index, h, i] = carry[h][i]


def own_kernel(
    own_cols,
    pad,
    radius,
    own_ref,
    field_ref,
    take_ref,
    acc_ref,
    second_ref,
    state_ref,
    image_ref,
    carry_ref,
    table_ref,
):
    shell = Shell(own_cols, pad, radius, field_ref, take_ref, acc_ref, state_ref, table_ref)
    for col in range(pad, pad + own_cols):
        for i in range(3, 6):
            start = col * SUBS * SUBS + i * SUBS
            field_ref[start : start + SUBS, :] = shell.zero
    shell.spread(own_ref, pad, own_cols)
    stop = pad + own_cols

    def state(col, index):
        return shell.field(col, (0, 1, 2, 6)[index])

    def direction(col, index):
        return shell.field(col, 3 + index)

    def image(col, index):
        return image_ref[0, col, index]

    keep(carry_ref, 0, shell.axial_take(pad, stop, state, 0, shell.nothing, thick=True))
    keep(carry_ref, 1, shell.axial_take(pad, stop, direction, VECTOR, shell.nothing))
    shell.prepare(pad, stop - 3)
    shell.clear(pad)
    shell.spans(pad, stop - 3)
    column = attached(own_ref, pad)
    shell.stringer(column, [shell.line_state(column, h) for h in range(2)])
    shell.gather(pad + 3, stop - 3, direction, image_ref, 0)

    keep(carry_ref, 2, shell.axial_take(pad + 3, stop - 3, image, VECTOR, shell.nothing))
    shell.acc_ref = second_ref
    shell.clear(pad + 3)
    shell.spans(pad + 3, stop - 6)


def krylov_kernel(
    own_cols,
    pad,
    radius,
    left_ref,
    right_ref,
    own_ref,
    carry_ref,
    field_in,
    take_in,
    acc_in,
    second_in,
    state_in,
    image_in,
    krylov_ref,
    gram_ref,
    field_ref,
    take_ref,
    acc_ref,
    second_ref,
    state_ref,
    image_ref,
    table_ref,
    line_ref,
):
    shell = Shell(own_cols, pad, radius, field_ref, take_ref, acc_ref, state_ref, table_ref)
    field, zero = shell.field, shell.zero
    stop = pad + own_cols
    shell.spread(left_ref, pad - HALO, HALO)
    shell.spread(right_ref, stop, HALO)

    def carried(index):
        return tuple(tuple(carry_ref[index, h, i] for i in range(5)) for h in range(2))

    def state(col, index):
        return field(col, (0, 1, 2, 6)[index])

    def vector(step):
        def load(col, index):
            if step == 0:
                return field(col, 3 + index)
            return image_ref[step - 1, col, index]

        return load

    shell.axial_take(pad - HALO, pad + 2, state, 0, shell.nothing, thick=True)
    shell.axial_take(stop, stop + HALO, state, 0, carried(0), thick=True)
    shell.prepare(pad - HALO, pad)
    shell.prepare(stop - 3, stop + HALO - 3)
    stringers = [
        attached(source, pad + (i - 1) * own_cols)
        for i, source in enumerate((left_ref, own_ref, right_ref))
    ]
    for i, column in enumerate(stringers):
        for h in range(2):
            line_ref[i, h, 0], line_ref[i, h, 1] = shell.line_state(column, h)

    def add_stringers(which):
        for i in which:
            shell.stringer(
                stringers[i], [(line_ref[i, h, 0], line_ref[i, h, 1]) for h in range(2)]
            )

    low, high = pad, stop
    for step in range(STEPS):
        reach = HALO - 3 * step
        first, last = pad - reach, stop + reach - 3
        load = vector(step)
        if step < 2:
            shell.acc_ref = (acc_ref, second_ref)[step]
            shell.axial_take(first, low + 2, load, VECTOR, shell.nothing)
            shell.axial_take(high, last + 3, load, VECTOR, carried(1 + step))
            shell.clear(first, low - first)
            shell.spans(first, low, fresh=False)
            shell.spans(high - 3, last)
            low, high = low + 3, high - 3
        else:
            shell.acc_ref = acc_ref
            shell.axial_take(first, last + 3, load, VECTOR, shell.nothing)
            shell.clear(first)
            shell.spans(first, last)
        if step == 0:
            add_stringers((0, 2))
            shell.gather(first + 3, low, load, image_ref, step)
            shell.gather(high, last, load, image_ref, step)
        else:
            add_stringers(range(3))
            shell.gather(first + 3, last, load, image_ref, step)

    def inner(cols, sums):
        sums = list(sums)
        for col in cols:
            for comp in range(3):
                vectors = [field(pad + col, 3 + comp)] + [
                    image_ref[s, pad + col, comp] for s in range(STEPS)
                ]
                for s, vector in enumerate(vectors):
                    start = pl.multiple_of(col * (3 * SUBS) + comp * SUBS, SUBS)
                    krylov_ref[s, pl.ds(start, SUBS), :] = vector
                for n, (x, y) in enumerate(PAIRS):
                    sums[n] = sums[n] + vectors[x] * vectors[y]
        return tuple(sums)

    sums = loop(0, own_cols, inner, (zero,) * len(PAIRS), 4)
    row = jnp.zeros((1, LANES), jnp.float32)
    for n, s in enumerate(sums):
        part = jnp.sum(jnp.sum(s, axis=0, keepdims=True), axis=1, keepdims=True)
        row = jnp.where(shell.lane[0:1] == n, part, row)
    gram_ref[...] = jnp.broadcast_to(row, gram_ref.shape)


def combine_kernel(count_all, gram_ref, krylov_ref, vectors_ref, alpha_ref, beta_ref):
    row = jnp.sum(gram_ref[...], axis=0, keepdims=True) * (1.0 / count_all)
    gram = {}
    for n, (i, j) in enumerate(PAIRS):
        gram[i, j] = gram[j, i] = row[:, n : n + 1]

    def product(x, y):
        return sum(x[i] * (sum(gram[i, j] * y[j] for j in range(len(y)))) for i in range(len(x)))

    def raised(x):
        return [jnp.zeros_like(x[0])] + x

    def less(x, scale, y):
        return [
            x[i] - scale * y[i] if i < len(y) else x[i] for i in range(len(x))
        ]

    current = [jnp.ones((1, 1), jnp.float32)]
    previous = None
    square = product(current, current) + EPSILON
    scale = square
    alphas, polynomials, scales, betas = [], [], [], []
    for step in range(STEPS):
        image = raised(current)
        alpha = product(current, image) / scale
        following = less(image, alpha, current)
        if previous is not None:
            following = less(following, square, previous)
        previous, current = current, following
        square = product(current, current) / scale + EPSILON
        scale = scale * square
        alphas.append(alpha)
        betas.append(square)
        polynomials.append(current)
        scales.append(scale)
    root = jnp.sqrt(jnp.concatenate(betas, axis=0))
    inverse = [1.0 / jnp.sqrt(s) for s in scales]
    for s in range(STEPS):
        alpha_ref[s] = jnp.max(alphas[s])
        beta_ref[s] = jnp.max(root[s : s + 1, :])
    factors = [
        [jnp.broadcast_to(c * inverse[s], (SUBS, LANES)) for c in polynomials[s]]
        for s in range(STEPS)
    ]
    own_cols, length = vectors_ref.shape[2], vectors_ref.shape[3]
    for comp in range(3):
        for block in range(own_cols // SUBS):
            for c in range((length + LANES - 1) // LANES):
                start = block * SUBS * 3 * SUBS + comp * SUBS + c
                vectors = [
                    krylov_ref[s, pl.ds(start, SUBS, stride=3 * SUBS), :] for s in range(STEPS + 1)
                ]
                width = min(LANES, length - c * LANES)
                for s in range(STEPS):
                    result = sum(factors[s][i] * vectors[i] for i in range(s + 2))
                    vectors_ref[
                        s, comp, block * SUBS : (block + 1) * SUBS, c * LANES : c * LANES + width
                    ] = result[:, :width]


def per_device(state_field, direction, skin_thickness, stringer_column):
    count = lax.axis_size("circ")
    own_cols, axial_count = state_field.shape[1:]
    radius = own_cols * count / (2.0 * math.pi)
    count_all = 3.0 * own_cols * axial_count * count
    pad = own_cols
    chunks = -(-axial_count // LANES)
    columns = 3 * own_cols
    vmem = pl.BlockSpec(memory_space=pltpu.VMEM)
    smem = pl.BlockSpec(memory_space=pltpu.SMEM)

    def shape(*dims):
        return jax.ShapeDtypeStruct(dims, jnp.float32)

    def params(mebibytes):
        return pltpu.CompilerParams(vmem_limit_bytes=mebibytes * 1024 * 1024)

    fields = jnp.concatenate([state_field, direction, skin_thickness[None]], axis=0)
    packed, head, tail = pl.pallas_call(
        functools.partial(pack_kernel, own_cols),
        out_shape=(
            shape(chunks * own_cols * SUBS, LANES),
            shape(chunks * HALO * SUBS, LANES),
            shape(chunks * HALO * SUBS, LANES),
        ),
        in_specs=[vmem, smem],
        out_specs=(vmem,) * 3,
        compiler_params=params(8),
        name="pack",
    )(fields, stringer_column)
    left = lax.ppermute(tail, "circ", [(i, (i + 1) % count) for i in range(count)])
    right = lax.ppermute(head, "circ", [((i + 1) % count, i) for i in range(count)])
    buffers = (
        shape(columns * SUBS * SUBS, LANES),
        shape(21, columns, 2, SUBS, LANES),
        shape(10, columns, 2, SUBS, LANES),
        shape(10, columns, 2, SUBS, LANES),
        shape(columns, 2, 4, 8, SUBS, LANES),
        shape(STEPS, columns, 3, SUBS, LANES),
    )
    table = pltpu.VMEM((2, 9, SUBS, LANES), jnp.float32)
    *kept, carry = pl.pallas_call(
        functools.partial(own_kernel, own_cols, pad, radius),
        out_shape=buffers + (shape(3, 2, 5, SUBS, LANES),),
        in_specs=[vmem],
        out_specs=(vmem,) * 7,
        scratch_shapes=[table],
        compiler_params=params(4),
        cost_estimate=pl.CostEstimate(flops=40000000, bytes_accessed=20000000, transcendentals=0),
        name="own",
    )(packed)
    krylov, gram, *_ = pl.pallas_call(
        functools.partial(krylov_kernel, own_cols, pad, radius),
        out_shape=(shape(STEPS + 1, own_cols * 3 * SUBS, LANES), shape(count, LANES)) + buffers,
        in_specs=[vmem] * 10,
        out_specs=(vmem,) * 8,
        input_output_aliases={4 + i: 2 + i for i in range(len(buffers))},
        scratch_shapes=[
            table,
            pltpu.VMEM((3, 2, 2, SUBS, LANES), jnp.float32),
        ],
        compiler_params=params(8),
        name="krylov",
    )(left, right, packed, carry, *kept)
    gram = lax.all_to_all(gram, "circ", 0, 0, tiled=True)
    return pl.pallas_call(
        functools.partial(combine_kernel, count_all),
        out_shape=(shape(STEPS, 3, own_cols, axial_count), shape(STEPS), shape(STEPS)),
        in_specs=[vmem] * 2,
        out_specs=(vmem, smem, smem),
        compiler_params=params(8),
        name="combine",
    )(gram, krylov)


def solution(mesh):
    in_specs = (P("group", "circ", None), P("group", "circ", None), P("circ", None), P("circ"))
    out_specs = (P("group", None, "circ", None), P("group"), P("group"))
    return jax.shard_map(
        per_device, mesh=mesh, in_specs=in_specs, out_specs=out_specs, check_vma=False
    )
```

```python
import functools
import math

import jax
import jax.numpy as jnp
from jax import lax
from jax.experimental import pallas as pl
from jax.experimental.pallas import tpu as pltpu
from jax.sharding import PartitionSpec as P

STEPS = 3

POISSON = 0.3
EPSILON = 1e-06
STRINGER_AXIAL = 40.0
STRINGER_BENDING = 20.0
END_STIFF = 4.0

LANES = 128
SUBS = 8
HALF = 4
HALO = 3 * STEPS

A1, B1, C0, C1, C2, DA0, DB0, DC0, DC1, DDC0, H0 = range(11)
F01, F00, F10, F11, F20, F20Q, F20L, F21, F21Q, F22 = range(10)
S_WX, S_WS, S_NX, S_NS, S_NG, S_A, S_AG, S_D = range(8)


def gauss_rule():
    inner_root = math.sqrt(3.0 / 7.0 - 2.0 / 7.0 * math.sqrt(6.0 / 5.0))
    outer_root = math.sqrt(3.0 / 7.0 + 2.0 / 7.0 * math.sqrt(6.0 / 5.0))
    weight_inner = (18.0 + math.sqrt(30.0)) / 72.0
    weight_outer = (18.0 - math.sqrt(30.0)) / 72.0
    points = [
        0.5 - 0.5 * outer_root,
        0.5 - 0.5 * inner_root,
        0.5 + 0.5 * inner_root,
        0.5 + 0.5 * outer_root,
    ]
    return points, [weight_outer, weight_inner, weight_inner, weight_outer]


def cubic(t):
    s = 1.0 - t
    return [
        s**3 / 6.0,
        (3.0 * t**3 - 6.0 * t**2 + 4.0) / 6.0,
        (-3.0 * t**3 + 3.0 * t**2 + 3.0 * t + 1.0) / 6.0,
        t**3 / 6.0,
    ]


def quadratic(t):
    return [(1.0 - t) ** 2 / 2.0, -(t**2) + t + 0.5, t**2 / 2.0]


POINTS, WEIGHTS = gauss_rule()


def take4(z):
    p03, m03, p12, m12 = z[0] + z[3], z[0] - z[3], z[1] + z[2], z[1] - z[2]
    rest = p03 - p12

    def at(t, scale=1.0):
        b = [scale * x for x in cubic(t)]
        whole = p12 if scale == 1.0 else p12 * scale
        return whole + rest * (b[0] + b[3]), m03 * (b[0] - b[3]) + m12 * (b[1] - b[2])

    return at


def take3(d):
    p, m = d[0] + d[2], d[0] - d[2]

    def at(t, scale=1.0):
        q = [2.0 * scale * x for x in quadratic(t)]
        return p * (0.5 * (q[0] + q[2])) + d[1] * q[1], m * (0.5 * (q[0] - q[2]))

    return at


def take2(g):
    even, m = g[0] + g[1], g[0] - g[1]

    def at(t):
        return even, m * (1.0 - 2.0 * t)

    return at


def both(pair):
    return pair[0] + pair[1], pair[0] - pair[1]


def merged(first, second):
    return first[0] + second[0], first[1] + second[1]


def put4(pairs, scale=1.0):
    total, sums = None, None
    for t, (one, two) in pairs:
        s, d = one + two, one - two
        b = [scale * x for x in cubic(t)]
        total = s if total is None else total + s
        terms = [s * (b[0] + b[3]), d * (b[0] - b[3]), d * (b[1] - b[2])]
        sums = terms if sums is None else [x + y for x, y in zip(sums, terms)]
    e03, o03, o12 = sums
    e12 = (total if scale == 1.0 else total * scale) - e03
    return [e03 + o03, e12 + o12, e12 - o12, e03 - o03]


def put3(pairs):
    sums = None
    for t, (one, two) in pairs:
        s, d = one + two, one - two
        q = [2.0 * x for x in quadratic(t)]
        terms = [s * (0.5 * (q[0] + q[2])), d * (0.5 * (q[0] - q[2])), s * q[1]]
        sums = terms if sums is None else [x + y for x, y in zip(sums, terms)]
    even, odd, middle = sums
    return [even + odd, middle, even - odd]


def put2(pairs):
    even, odd = None, None
    for t, (one, two) in pairs:
        s, d = one + two, (one - two) * (1.0 - 2.0 * t)
        even = s if even is None else even + s
        odd = d if odd is None else odd + d
    return [even + odd, even - odd]


VECTOR = 11
MARKS = (2.0 / 6.0, 8.0 / 6.0, 2.0 / 6.0)
TAPS = ((F01, 4), (F00, 3), (F10, 3), (F11, 4), (F20, 4), (F20Q, 3), (F20L, 2), (F21, 4), (F21Q, 3), (F22, 4))
PAIRS = [(i, j) for i in range(STEPS + 1) for j in range(i, STEPS + 1)]


def loop(low, high, body, carry, unroll=1):
    rounds = (high - low) // unroll

    def several(i, carry):
        start = low + i * unroll
        return body([start + u for u in range(unroll)], carry)

    if rounds > 0:
        carry = lax.fori_loop(0, rounds, several, carry)
    rest = list(range(low + rounds * unroll, high))
    return body(rest, carry) if rest else carry


def pack_kernel(own_cols, fields_ref, column_ref, own_ref, head_ref, tail_ref):
    length = fields_ref.shape[2]
    chunks = own_ref.shape[0] // (own_cols * SUBS)
    local = lax.rem(column_ref[0], own_cols).astype(jnp.float32)

    def put(f, rows, part, c):
        own_ref[pl.ds((c * own_cols + rows) * SUBS + f, SUBS, stride=SUBS), :] = part
        for ref, low in ((head_ref, 0), (tail_ref, own_cols - HALO)):
            start, stop = max(rows, low), min(rows + SUBS, low + HALO)
            if stop - start == SUBS:
                row = (c * HALO + start - low) * SUBS + f
                ref[pl.ds(row, SUBS, stride=SUBS), :] = part
            else:
                for col in range(start, stop):
                    row = (c * HALO + col - low) * SUBS + f
                    ref[row : row + 1, :] = part[col - rows : col - rows + 1]

    for rows in range(0, own_cols, SUBS):
        for f in range(7):
            for c in range(chunks):
                width = min(LANES, length - c * LANES)
                part = fields_ref[f, rows : rows + SUBS, c * LANES : c * LANES + width]
                if width < LANES:
                    fill = jnp.zeros((SUBS, LANES - width), jnp.float32)
                    part = jnp.concatenate([part, fill], axis=1)
                put(f, rows, part, c)
        put(7, rows, jnp.full((SUBS, LANES), local), 0)


class Shell:
    def __init__(self, own_cols, pad, radius, field_ref, take_ref, acc_ref, state_ref, table_ref):
        self.own_cols, self.pad, self.radius = own_cols, pad, radius
        self.field_ref, self.take_ref, self.acc_ref = field_ref, take_ref, acc_ref
        self.state_ref, self.table_ref = state_ref, table_ref
        self.sub = lax.broadcasted_iota(jnp.int32, (SUBS, LANES), 0)
        self.lane = lax.broadcasted_iota(jnp.int32, (SUBS, LANES), 1)
        self.low = self.sub < HALF
        row = jnp.where(self.lane == 1, 4.0, jnp.where(self.lane < 3, 1.0, 0.0))
        self.ends = jnp.where((self.sub == 0) | (self.sub == HALF), row, 0.0)
        self.zero = jnp.zeros((SUBS, LANES), jnp.float32)
        self.nothing = tuple((self.zero,) * 5 for _ in range(2))
        for h in range(2):
            first, second = POINTS[h], POINTS[3 - h]
            rows = (
                list(zip(cubic(first), cubic(second)))
                + list(zip(quadratic(first), quadratic(second)))
                + [(1.0 - first, 1.0 - second), (first, second)]
            )
            for i, (x, y) in enumerate(rows):
                table_ref[h, i] = jnp.where(self.low, jnp.float32(0.5 * x), jnp.float32(0.5 * y))

    def spread(self, source, offset, count):
        for c in range(source.shape[0] // (count * SUBS)):
            for i in range(count):
                start = (offset + i) * SUBS * SUBS + c
                row = (c * count + i) * SUBS
                self.field_ref[pl.ds(start, SUBS, stride=SUBS), :] = source[row : row + SUBS, :]

    def field(self, col, index):
        start = col * (SUBS * SUBS) + index * SUBS
        if not isinstance(start, int):
            start = pl.multiple_of(start, SUBS)
        return self.field_ref[pl.ds(start, SUBS), :]

    def shifted(self, v):
        following = pltpu.roll(v, SUBS - 1, 0)
        shifts = [v] + [
            pltpu.roll(jnp.where(self.lane < o, following, v), LANES - o, 1) for o in range(1, 4)
        ]
        return [jnp.where(self.low, z, pltpu.roll(z, HALF, 0)) for z in shifts]

    def value(self, z, h):
        return sum(self.table_ref[h, o] * z[o] for o in range(4))

    def slope(self, d, h):
        return sum(self.table_ref[h, 4 + o] * d[o] for o in range(3))

    def curve(self, g, h):
        return self.table_ref[h, 7] * g[0] + self.table_ref[h, 8] * g[1]

    def take_columns(self, cols, load, base, carry, thick=False):
        take_ref = self.take_ref

        def differences(z):
            return [z[o + 1] - z[o] for o in range(len(z) - 1)]

        loaded = [[load(col, i) for i in range(4 if thick else 3)] for col in cols]
        for col, vectors in zip(cols, loaded):
            za, zb, zc = (self.shifted(v) for v in vectors[:3])
            da, db, dc = differences(za), differences(zb), differences(zc)
            gc = differences(dc)
            zh = self.shifted(vectors[3]) if thick else None
            out = []
            for h in range(2):
                old_a0, old_b0, old_c0, old_c1, old_dc0 = carry[h]
                a0, b0, c0 = self.value(za, h), self.value(zb, h), self.value(zc, h)
                c1, dc0 = self.slope(dc, h), c0 - old_c0
                take_ref[base + A1, col, h] = self.slope(da, h)
                take_ref[base + B1, col, h] = self.slope(db, h)
                take_ref[base + C0, col, h] = c0
                take_ref[base + C1, col, h] = c1
                take_ref[base + DA0, col - 1, h] = a0 - old_a0
                take_ref[base + DB0, col - 1, h] = b0 - old_b0
                take_ref[base + DC0, col - 1, h] = dc0
                if thick:
                    take_ref[base + H0, col, h] = self.value(zh, h)
                else:
                    take_ref[base + C2, col, h] = self.curve(gc, h)
                    take_ref[base + DC1, col - 1, h] = c1 - old_c1
                    take_ref[base + DDC0, col - 2, h] = dc0 - old_dc0
                out.append((a0, b0, c0, c1, dc0))
            carry = tuple(out)
        return carry

    def axial_take(self, low, high, load, base, carry, thick=False, unroll=4):
        def body(cols, carry):
            return self.take_columns(cols, load, base, carry, thick)

        return loop(low, high, body, carry, unroll)

    def takes(self, name, k, h, taps):
        return [self.take_ref[name, k + o, h] for o in range(taps)]

    def prepare(self, low, high):
        inverse = 1.0 / (1.0 - POISSON * POISSON)
        takes, state_ref = self.takes, self.state_ref

        def body(cols, unused):
            (k,) = cols
            for h in range(2):
                u1 = take4(takes(A1, k, h, 4))
                us = take3(takes(DA0, k, h, 3))
                vs = take3(takes(DB0, k, h, 3))
                vx = take4(takes(B1, k, h, 4))
                w0 = take4(takes(C0, k, h, 4))
                w1 = take4(takes(C1, k, h, 4))
                ws = take3(takes(DC0, k, h, 3))
                h0 = take4(takes(H0, k, h, 4))
                for p in range(2):
                    t = POINTS[p]
                    weight = WEIGHTS[p] * WEIGHTS[h]
                    along = both(u1(t))
                    across = both(merged(vs(t), w0(t, 1.0 / self.radius)))
                    shear = both(merged(us(t), vx(t)))
                    tilt_x, tilt_s, thick = both(w1(t)), both(ws(t)), both(h0(t))
                    for q in range(2):
                        wx, wc, th = tilt_x[q], tilt_s[q], thick[q]
                        ex = along[q] + 0.5 * wx * wx
                        es = across[q] + 0.5 * wc * wc
                        g = shear[q] + wx * wc
                        a = th * (inverse * weight)
                        ag = a * (0.5 * (1.0 - POISSON))
                        point = p if q == 0 else 3 - p
                        state_ref[k, h, point, S_WX] = wx
                        state_ref[k, h, point, S_WS] = wc
                        state_ref[k, h, point, S_NX] = a * (ex + POISSON * es)
                        state_ref[k, h, point, S_NS] = a * (POISSON * ex + es)
                        state_ref[k, h, point, S_NG] = ag * g
                        state_ref[k, h, point, S_A] = a
                        state_ref[k, h, point, S_AG] = ag
                        state_ref[k, h, point, S_D] = a * (th * th) * (1.0 / 12.0)
            return unused

        loop(low, high, body, 0)

    def clear(self, low, count=None):
        for name, taps in TAPS:
            for o in range(taps - 1 if count is None else count):
                for h in range(2):
                    self.acc_ref[name, low + o, h] = self.zero

    def spans(self, low, high, fresh=True):
        takes, state_ref, acc_ref = self.takes, self.state_ref, self.acc_ref

        def add(name, k, h, parts):
            for o, part in enumerate(parts):
                if fresh and o == len(parts) - 1:
                    acc_ref[name, k + o, h] = part
                else:
                    acc_ref[name, k + o, h] += part

        def body(cols, unused):
            (k,) = cols
            for h in range(2):
                a1 = take4(takes(VECTOR + A1, k, h, 4))
                b1 = take4(takes(VECTOR + B1, k, h, 4))
                c0 = take4(takes(VECTOR + C0, k, h, 4))
                c1 = take4(takes(VECTOR + C1, k, h, 4))
                c2 = take4(takes(VECTOR + C2, k, h, 4))
                as0 = take3(takes(VECTOR + DA0, k, h, 3))
                bs0 = take3(takes(VECTOR + DB0, k, h, 3))
                cs0 = take3(takes(VECTOR + DC0, k, h, 3))
                cx0 = take3(takes(VECTOR + DC1, k, h, 3))
                cc0 = take2(takes(VECTOR + DDC0, k, h, 2))
                parts = []
                for p in range(2):
                    t = POINTS[p]
                    along = both(a1(t))
                    across = both(merged(bs0(t), c0(t, 1.0 / self.radius)))
                    shear = both(merged(as0(t), b1(t)))
                    tilt_x, tilt_s = both(c1(t)), both(cs0(t))
                    bend_x, bend_s = both(c2(t)), both(cc0(t))
                    twist = both(cx0(t, 2.0 * (1.0 - POISSON)))
                    results = []
                    for q in range(2):
                        point = p if q == 0 else 3 - p
                        wx, wc = state_ref[k, h, point, S_WX], state_ref[k, h, point, S_WS]
                        cx, cs = tilt_x[q], tilt_s[q]
                        ex = along[q] + wx * cx
                        es = across[q] + wc * cs
                        g = shear[q] + wx * cs + wc * cx
                        a = state_ref[k, h, point, S_A]
                        fx = a * (ex + POISSON * es)
                        fs = a * (POISSON * ex + es)
                        fg = state_ref[k, h, point, S_AG] * g
                        d = state_ref[k, h, point, S_D]
                        mx = d * (bend_x[q] + POISSON * bend_s[q])
                        ms = d * (POISSON * bend_x[q] + bend_s[q])
                        mg = d * twist[q]
                        ng = state_ref[k, h, point, S_NG]
                        sx = fx * wx + fg * wc + state_ref[k, h, point, S_NX] * cx + ng * cs
                        ss = fs * wc + fg * wx + state_ref[k, h, point, S_NS] * cs + ng * cx
                        results.append((fx, fs, fg, mx, ms, mg, sx, ss))
                    parts.append((t, list(zip(*results))))

                def pick(i):
                    return [(t, values[i]) for t, values in parts]

                add(F01, k, h, put4(pick(0)))
                add(F00, k, h, put3(pick(2)))
                add(F10, k, h, put3(pick(1)))
                add(F11, k, h, put4(pick(2)))
                add(F20, k, h, put4(pick(1), 1.0 / self.radius))
                add(F20Q, k, h, put3(pick(7)))
                add(F20L, k, h, put2(pick(4)))
                add(F21, k, h, put4(pick(6)))
                add(F21Q, k, h, put3(pick(5)))
                add(F22, k, h, put4(pick(3)))
            return unused

        loop(low, high, body, 0)

    def axial_put(self, zeroth, first, second):
        table_ref, lane, low = self.table_ref, self.lane, self.low
        t = [sum(table_ref[h, o] * zeroth[h] for h in range(2)) for o in range(4)]
        r = [sum(table_ref[h, 4 + o] * first[h] for h in range(2)) for o in range(3)]
        t = [t[0] - r[0], t[1] + (r[0] - r[1]), t[2] + (r[1] - r[2]), t[3] + r[2]]
        if second is not None:
            l0, l1 = (sum(table_ref[h, 7 + o] * second[h] for h in range(2)) for o in range(2))
            t = [t[0] + l0, t[1] + (l1 - 2.0 * l0), t[2] + (l0 - 2.0 * l1), t[3] + l1]
        stay, cross = t[0], self.zero
        for o in range(1, 4):
            moved = pltpu.roll(t[o], o, 1)
            stay = stay + jnp.where(lane < o, 0.0, moved)
            cross = cross + jnp.where(lane < o, moved, 0.0)
        stay = jnp.where(low, stay + pltpu.roll(stay, HALF, 0), 0.0)
        cross = jnp.where(low, cross + pltpu.roll(cross, HALF, 0), 0.0)
        return stay + pltpu.roll(cross, 1, 0)

    def end_part(self, v):
        total = jnp.sum(v * self.ends, axis=1, keepdims=True)
        return (total * (END_STIFF / 36.0)) * self.ends

    def line(self, name, column, h):
        return sum(MARKS[j] * self.take_ref[name, column + j, h] for j in range(3))

    def line_state(self, column, h):
        along, tilt = self.line(A1, column, h), self.line(C1, column, h)
        return along + 0.5 * tilt * tilt, tilt

    def stringer(self, column, states):
        for h in range(2):
            weight = jnp.float32(WEIGHTS[h])
            stretch, tilt = states[h]
            slope_c = self.line(VECTOR + C1, column, h)
            d_stretch = self.line(VECTOR + A1, column, h) + tilt * slope_c
            f0 = (STRINGER_AXIAL * weight) * d_stretch
            f1 = (STRINGER_AXIAL * weight) * (d_stretch * tilt + stretch * slope_c)
            f2 = (STRINGER_BENDING * weight) * self.line(VECTOR + C2, column, h)
            for j in range(3):
                self.acc_ref[F01, column + j, h] += MARKS[j] * f0
                self.acc_ref[F21, column + j, h] += MARKS[j] * f1
                self.acc_ref[F22, column + j, h] += MARKS[j] * f2

    def image_columns(self, cols, load):
        acc_ref, halves = self.acc_ref, range(2)

        def back(name, col, h):
            return acc_ref[name, col - 1, h] - acc_ref[name, col, h]

        work = []
        for col in cols:
            zeroth = [
                [back(F00, col, h) for h in halves],
                [back(F10, col, h) for h in halves],
                [
                    acc_ref[F20, col, h]
                    + back(F20Q, col, h)
                    + (acc_ref[F20L, col - 2, h] - acc_ref[F20L, col - 1, h])
                    - back(F20L, col, h)
                    for h in halves
                ],
            ]
            first = [
                [acc_ref[F01, col, h] for h in halves],
                [acc_ref[F11, col, h] for h in halves],
                [acc_ref[F21, col, h] + back(F21Q, col, h) for h in halves],
            ]
            second = [None, None, [acc_ref[F22, col, h] for h in halves]]
            work.append((zeroth, first, second, [load(col, i) for i in range(3)]))
        return [
            [
                self.axial_put(zeroth[i], first[i], second[i]) + self.end_part(v[i])
                for i in range(3)
            ]
            for zeroth, first, second, v in work
        ]

    def gather(self, low, high, load, image_ref, step, follow, carry, unroll, beyond=0):
        count = high - low
        ahead = min(count, unroll + count % unroll)

        def put(cols, images):
            for col, image in zip(cols, images):
                for i in range(3):
                    image_ref[step, col, i] = image[i]

        def body(start, carry):
            cols = [start + ahead + u for u in range(unroll)]
            images = self.image_columns(cols, load)
            carry = follow([start + u for u in range(unroll)], carry)
            put(cols, images)
            return carry

        cols = list(range(low, low + ahead))
        put(cols, self.image_columns(cols, load))
        rounds = (count - ahead) // unroll
        if rounds > 0:
            carry = lax.fori_loop(0, rounds, lambda i, c: body(low + i * unroll, c), carry)
        return follow(list(range(low + rounds * unroll, high + beyond)), carry)


def attached(source, shift):
    return jnp.max(source[7:8, :]).astype(jnp.int32) + shift


def keep(ref, index, carry):
    for h in range(2):
        for i in range(5):
            ref[index, h, i] = carry[h][i]


def own_kernel(
    own_cols,
    pad,
    radius,
    own_ref,
    field_ref,
    take_ref,
    acc_ref,
    second_ref,
    state_ref,
    image_ref,
    carry_ref,
    table_ref,
):
    shell = Shell(own_cols, pad, radius, field_ref, take_ref, acc_ref, state_ref, table_ref)
    for col in range(pad, pad + own_cols):
        for i in range(3, 6):
            start = col * SUBS * SUBS + i * SUBS
            field_ref[start : start + SUBS, :] = shell.zero
    shell.spread(own_ref, pad, own_cols)
    stop = pad + own_cols

    def state(col, index):
        return shell.field(col, (0, 1, 2, 6)[index])

    def direction(col, index):
        return shell.field(col, 3 + index)

    def image(col, index):
        return image_ref[0, col, index]

    keep(carry_ref, 0, shell.axial_take(pad, stop, state, 0, shell.nothing, thick=True))
    keep(carry_ref, 1, shell.axial_take(pad, stop, direction, VECTOR, shell.nothing))
    shell.prepare(pad, stop - 3)
    shell.clear(pad)
    shell.spans(pad, stop - 3)
    column = attached(own_ref, pad)
    shell.stringer(column, [shell.line_state(column, h) for h in range(2)])

    def follow(cols, carry):
        return shell.take_columns(cols, image, VECTOR, carry)

    carry = shell.gather(
        pad + 3, stop - 3, direction, image_ref, 0, follow, shell.nothing, unroll=3
    )
    keep(carry_ref, 2, carry)
    shell.acc_ref = second_ref
    shell.clear(pad + 3)
    shell.spans(pad + 3, stop - 6)


def krylov_kernel(
    own_cols,
    pad,
    radius,
    left_ref,
    right_ref,
    own_ref,
    carry_ref,
    field_in,
    take_in,
    acc_in,
    second_in,
    state_in,
    image_in,
    krylov_ref,
    gram_ref,
    field_ref,
    take_ref,
    acc_ref,
    second_ref,
    state_ref,
    image_ref,
    table_ref,
    line_ref,
):
    shell = Shell(own_cols, pad, radius, field_ref, take_ref, acc_ref, state_ref, table_ref)
    field, zero = shell.field, shell.zero
    stop = pad + own_cols
    shell.spread(left_ref, pad - HALO, HALO)
    shell.spread(right_ref, stop, HALO)

    def carried(index):
        return tuple(tuple(carry_ref[index, h, i] for i in range(5)) for h in range(2))

    def state(col, index):
        return field(col, (0, 1, 2, 6)[index])

    def vector(step):
        def load(col, index):
            if step == 0:
                return field(col, 3 + index)
            return image_ref[step - 1, col, index]

        return load

    shell.axial_take(pad - HALO, pad + 2, state, 0, shell.nothing, thick=True)
    shell.axial_take(stop, stop + HALO, state, 0, carried(0), thick=True)
    shell.prepare(pad - HALO, pad)
    shell.prepare(stop - 3, stop + HALO - 3)
    stringers = [
        attached(source, pad + (i - 1) * own_cols)
        for i, source in enumerate((left_ref, own_ref, right_ref))
    ]
    for i, column in enumerate(stringers):
        for h in range(2):
            line_ref[i, h, 0], line_ref[i, h, 1] = shell.line_state(column, h)

    def add_stringers(which):
        for i in which:
            shell.stringer(
                stringers[i], [(line_ref[i, h, 0], line_ref[i, h, 1]) for h in range(2)]
            )

    def take_next(step):
        load = vector(step + 1)
        return lambda cols, carry: shell.take_columns(cols, load, VECTOR, carry)

    def inner(cols, sums):
        sums = list(sums)
        for col in cols:
            for comp in range(3):
                vectors = [vector(s)(col, comp) for s in range(STEPS + 1)]
                for s, x in enumerate(vectors):
                    start = (col - pad) * (3 * SUBS) + comp * SUBS
                    if not isinstance(start, int):
                        start = pl.multiple_of(start, SUBS)
                    krylov_ref[s, pl.ds(start, SUBS), :] = x
                for n, (i, j) in enumerate(PAIRS):
                    sums[n] = sums[n] + vectors[i] * vectors[j]
        return tuple(sums)

    for step in range(STEPS):
        reach = HALO - 3 * step
        first, last = pad - reach, stop + reach - 3
        low, high = pad + 3 * step, stop - 3 * step
        load = vector(step)
        if step == 0:
            shell.axial_take(first, low + 2, load, VECTOR, shell.nothing)
            shell.axial_take(high, last + 3, load, VECTOR, carried(1))
        shell.acc_ref = second_ref if step == 1 else acc_ref
        if step < 2:
            shell.clear(first, low - first)
            shell.spans(first, low, fresh=False)
            shell.spans(high - 3, last)
        else:
            shell.clear(first)
            shell.spans(first, last)
        add_stringers((0, 2) if step == 0 else (0, 1, 2))
        if step == 0:
            follow = take_next(step)
            shell.gather(
                first + 3, low + 3, load, image_ref, step, follow, shell.nothing, 3, beyond=2
            )
            shell.gather(high - 3, last, load, image_ref, step, follow, carried(2), 3)
        elif step < STEPS - 1:
            follow = take_next(step)
            shell.gather(first + 3, last, load, image_ref, step, follow, shell.nothing, 4)
        else:
            nothing = (zero,) * len(PAIRS)
            sums = shell.gather(pad, stop, load, image_ref, step, inner, nothing, 4)

    row = jnp.zeros((1, LANES), jnp.float32)
    for n, s in enumerate(sums):
        part = jnp.sum(jnp.sum(s, axis=0, keepdims=True), axis=1, keepdims=True)
        row = jnp.where(shell.lane[0:1] == n, part, row)
    gram_ref[...] = jnp.broadcast_to(row, gram_ref.shape)


def combine_kernel(count_all, gram_ref, krylov_ref, vectors_ref, alpha_ref, beta_ref):
    row = jnp.sum(gram_ref[...], axis=0, keepdims=True) * (1.0 / count_all)
    gram = {}
    for n, (i, j) in enumerate(PAIRS):
        gram[i, j] = gram[j, i] = row[:, n : n + 1]

    def product(x, y):
        return sum(x[i] * (sum(gram[i, j] * y[j] for j in range(len(y)))) for i in range(len(x)))

    def raised(x):
        return [jnp.zeros_like(x[0])] + x

    def less(x, scale, y):
        return [
            x[i] - scale * y[i] if i < len(y) else x[i] for i in range(len(x))
        ]

    current = [jnp.ones((1, 1), jnp.float32)]
    previous = None
    square = product(current, current) + EPSILON
    scale = square
    alphas, polynomials, scales, betas = [], [], [], []
    for step in range(STEPS):
        image = raised(current)
        alpha = product(current, image) / scale
        following = less(image, alpha, current)
        if previous is not None:
            following = less(following, square, previous)
        previous, current = current, following
        square = product(current, current) / scale + EPSILON
        scale = scale * square
        alphas.append(alpha)
        betas.append(square)
        polynomials.append(current)
        scales.append(scale)
    root = jnp.sqrt(jnp.concatenate(betas, axis=0))
    inverse = [1.0 / jnp.sqrt(s) for s in scales]
    for s in range(STEPS):
        alpha_ref[s] = jnp.max(alphas[s])
        beta_ref[s] = jnp.max(root[s : s + 1, :])
    factors = [
        [jnp.broadcast_to(c * inverse[s], (SUBS, LANES)) for c in polynomials[s]]
        for s in range(STEPS)
    ]
    own_cols, length = vectors_ref.shape[2], vectors_ref.shape[3]
    for comp in range(3):
        for block in range(own_cols // SUBS):
            for c in range((length + LANES - 1) // LANES):
                start = block * SUBS * 3 * SUBS + comp * SUBS + c
                vectors = [
                    krylov_ref[s, pl.ds(start, SUBS, stride=3 * SUBS), :] for s in range(STEPS + 1)
                ]
                width = min(LANES, length - c * LANES)
                for s in range(STEPS):
                    result = sum(factors[s][i] * vectors[i] for i in range(s + 2))
                    vectors_ref[
                        s, comp, block * SUBS : (block + 1) * SUBS, c * LANES : c * LANES + width
                    ] = result[:, :width]


def per_device(state_field, direction, skin_thickness, stringer_column):
    count = lax.axis_size("circ")
    own_cols, axial_count = state_field.shape[1:]
    radius = own_cols * count / (2.0 * math.pi)
    count_all = 3.0 * own_cols * axial_count * count
    pad = own_cols
    chunks = -(-axial_count // LANES)
    columns = 3 * own_cols
    vmem = pl.BlockSpec(memory_space=pltpu.VMEM)
    smem = pl.BlockSpec(memory_space=pltpu.SMEM)

    def shape(*dims):
        return jax.ShapeDtypeStruct(dims, jnp.float32)

    def params(mebibytes):
        return pltpu.CompilerParams(vmem_limit_bytes=mebibytes * 1024 * 1024)

    fields = jnp.concatenate([state_field, direction, skin_thickness[None]], axis=0)
    packed, head, tail = pl.pallas_call(
        functools.partial(pack_kernel, own_cols),
        out_shape=(
            shape(chunks * own_cols * SUBS, LANES),
            shape(chunks * HALO * SUBS, LANES),
            shape(chunks * HALO * SUBS, LANES),
        ),
        in_specs=[vmem, smem],
        out_specs=(vmem,) * 3,
        compiler_params=params(8),
        name="pack",
    )(fields, stringer_column)
    left = lax.ppermute(tail, "circ", [(i, (i + 1) % count) for i in range(count)])
    right = lax.ppermute(head, "circ", [((i + 1) % count, i) for i in range(count)])
    buffers = (
        shape(columns * SUBS * SUBS, LANES),
        shape(21, columns, 2, SUBS, LANES),
        shape(10, columns, 2, SUBS, LANES),
        shape(10, columns, 2, SUBS, LANES),
        shape(columns, 2, 4, 8, SUBS, LANES),
        shape(STEPS, columns, 3, SUBS, LANES),
    )
    table = pltpu.VMEM((2, 9, SUBS, LANES), jnp.float32)
    *kept, carry = pl.pallas_call(
        functools.partial(own_kernel, own_cols, pad, radius),
        out_shape=buffers + (shape(3, 2, 5, SUBS, LANES),),
        in_specs=[vmem],
        out_specs=(vmem,) * 7,
        scratch_shapes=[table],
        compiler_params=params(4),
        cost_estimate=pl.CostEstimate(flops=40000000, bytes_accessed=20000000, transcendentals=0),
        name="own",
    )(packed)
    krylov, gram, *_ = pl.pallas_call(
        functools.partial(krylov_kernel, own_cols, pad, radius),
        out_shape=(shape(STEPS + 1, own_cols * 3 * SUBS, LANES), shape(count, LANES)) + buffers,
        in_specs=[vmem] * 10,
        out_specs=(vmem,) * 8,
        input_output_aliases={4 + i: 2 + i for i in range(len(buffers))},
        scratch_shapes=[
            table,
            pltpu.VMEM((3, 2, 2, SUBS, LANES), jnp.float32),
        ],
        compiler_params=params(8),
        name="krylov",
    )(left, right, packed, carry, *kept)
    gram = lax.all_to_all(gram, "circ", 0, 0, tiled=True)
    return pl.pallas_call(
        functools.partial(combine_kernel, count_all),
        out_shape=(shape(STEPS, 3, own_cols, axial_count), shape(STEPS), shape(STEPS)),
        in_specs=[vmem] * 2,
        out_specs=(vmem, smem, smem),
        compiler_params=params(8),
        name="combine",
    )(gram, krylov)


def solution(mesh):
    in_specs = (P("group", "circ", None), P("group", "circ", None), P("circ", None), P("circ"))
    out_specs = (P("group", None, "circ", None), P("group"), P("group"))
    return jax.shard_map(
        per_device, mesh=mesh, in_specs=in_specs, out_specs=out_specs, check_vma=False
    )
```

```python
import functools
import math

import jax
import jax.numpy as jnp
from jax import lax
from jax.experimental import pallas as pl
from jax.experimental.pallas import tpu as pltpu
from jax.sharding import PartitionSpec as P

STEPS = 3

POISSON = 0.3
EPSILON = 1e-06
STRINGER_AXIAL = 40.0
STRINGER_BENDING = 20.0
END_STIFF = 4.0

LANES = 128
SUBS = 8
HALF = 4
HALO = 3 * STEPS

A1, B1, C0, C1, C2, DA0, DB0, DC0, DC1, DDC0, H0 = range(11)
F01, F00, F10, F11, F20, F20Q, F20L, F21, F21Q, F22 = range(10)
S_WX, S_WS, S_NX, S_NS, S_NG, S_A, S_AG, S_D = range(8)


def gauss_rule():
    inner_root = math.sqrt(3.0 / 7.0 - 2.0 / 7.0 * math.sqrt(6.0 / 5.0))
    outer_root = math.sqrt(3.0 / 7.0 + 2.0 / 7.0 * math.sqrt(6.0 / 5.0))
    weight_inner = (18.0 + math.sqrt(30.0)) / 72.0
    weight_outer = (18.0 - math.sqrt(30.0)) / 72.0
    points = [
        0.5 - 0.5 * outer_root,
        0.5 - 0.5 * inner_root,
        0.5 + 0.5 * inner_root,
        0.5 + 0.5 * outer_root,
    ]
    return points, [weight_outer, weight_inner, weight_inner, weight_outer]


def cubic(t):
    s = 1.0 - t
    return [
        s**3 / 6.0,
        (3.0 * t**3 - 6.0 * t**2 + 4.0) / 6.0,
        (-3.0 * t**3 + 3.0 * t**2 + 3.0 * t + 1.0) / 6.0,
        t**3 / 6.0,
    ]


def quadratic(t):
    return [(1.0 - t) ** 2 / 2.0, -(t**2) + t + 0.5, t**2 / 2.0]


POINTS, WEIGHTS = gauss_rule()


def take4(z):
    p03, m03, p12, m12 = z[0] + z[3], z[0] - z[3], z[1] + z[2], z[1] - z[2]
    rest = p03 - p12

    def at(t, scale=1.0):
        b = [scale * x for x in cubic(t)]
        whole = p12 if scale == 1.0 else p12 * scale
        return whole + rest * (b[0] + b[3]), m03 * (b[0] - b[3]) + m12 * (b[1] - b[2])

    return at


def take3(d):
    p, m = d[0] + d[2], d[0] - d[2]

    def at(t, scale=1.0):
        q = [2.0 * scale * x for x in quadratic(t)]
        return p * (0.5 * (q[0] + q[2])) + d[1] * q[1], m * (0.5 * (q[0] - q[2]))

    return at


def take2(g):
    even, m = g[0] + g[1], g[0] - g[1]

    def at(t):
        return even, m * (1.0 - 2.0 * t)

    return at


def both(pair):
    return pair[0] + pair[1], pair[0] - pair[1]


def merged(first, second):
    return first[0] + second[0], first[1] + second[1]


def put4(pairs, scale=1.0):
    total, sums = None, None
    for t, (one, two) in pairs:
        s, d = one + two, one - two
        b = [scale * x for x in cubic(t)]
        total = s if total is None else total + s
        terms = [s * (b[0] + b[3]), d * (b[0] - b[3]), d * (b[1] - b[2])]
        sums = terms if sums is None else [x + y for x, y in zip(sums, terms)]
    e03, o03, o12 = sums
    e12 = (total if scale == 1.0 else total * scale) - e03
    return [e03 + o03, e12 + o12, e12 - o12, e03 - o03]


def put3(pairs):
    sums = None
    for t, (one, two) in pairs:
        s, d = one + two, one - two
        q = [2.0 * x for x in quadratic(t)]
        terms = [s * (0.5 * (q[0] + q[2])), d * (0.5 * (q[0] - q[2])), s * q[1]]
        sums = terms if sums is None else [x + y for x, y in zip(sums, terms)]
    even, odd, middle = sums
    return [even + odd, middle, even - odd]


def put2(pairs):
    even, odd = None, None
    for t, (one, two) in pairs:
        s, d = one + two, (one - two) * (1.0 - 2.0 * t)
        even = s if even is None else even + s
        odd = d if odd is None else odd + d
    return [even + odd, even - odd]


VECTOR = 11
MARKS = (2.0 / 6.0, 8.0 / 6.0, 2.0 / 6.0)
TAPS = ((F01, 4), (F00, 3), (F10, 3), (F11, 4), (F20, 4), (F20Q, 3), (F20L, 2), (F21, 4), (F21Q, 3), (F22, 4))
PAIRS = [(i, j) for i in range(STEPS + 1) for j in range(i, STEPS + 1)]


def loop(low, high, body, carry, unroll=1):
    rounds = (high - low) // unroll

    def several(i, carry):
        start = low + i * unroll
        return body([start + u for u in range(unroll)], carry)

    if rounds > 0:
        carry = lax.fori_loop(0, rounds, several, carry)
    rest = list(range(low + rounds * unroll, high))
    return body(rest, carry) if rest else carry


REST, FIRST_REST, ABOVE = 3, 24, 64


def pack_kernel(own_cols, fields_ref, column_ref, own_ref, head_ref, tail_ref):
    length = fields_ref.shape[2]
    chunks = own_ref.shape[0] // (own_cols * SUBS)
    local = lax.rem(column_ref[0], own_cols).astype(jnp.float32)
    lane = lax.broadcasted_iota(jnp.int32, (SUBS, LANES), 1)

    def put(f, rows, part, c):
        own_ref[pl.ds((c * own_cols + rows) * SUBS + f, SUBS, stride=SUBS), :] = part
        if c == chunks - 1:
            return
        for ref, low in ((head_ref, 0), (tail_ref, own_cols - HALO)):
            start, stop = max(rows, low), min(rows + SUBS, low + HALO)
            if stop - start == SUBS:
                row = (c * HALO + start - low) * SUBS + f
                ref[pl.ds(row, SUBS, stride=SUBS), :] = part
            else:
                for col in range(start, stop):
                    row = (c * HALO + col - low) * SUBS + f
                    ref[row : row + 1, :] = part[col - rows : col - rows + 1]

    for rows in range(0, own_cols, SUBS):
        rests = jnp.where(lane < ABOVE, 0.0, local)
        for f in range(7):
            for c in range(chunks):
                width = min(LANES, length - c * LANES)
                part = fields_ref[f, rows : rows + SUBS, c * LANES : c * LANES + width]
                if width < LANES:
                    fill = jnp.zeros((SUBS, LANES - width), jnp.float32)
                    part = jnp.concatenate([part, fill], axis=1)
                    rests = rests + pltpu.roll(part, FIRST_REST - REST * f, 1)
                put(f, rows, part, c)
        put(7, rows, rests, 0)


class Shell:
    def __init__(self, own_cols, pad, radius, field_ref, take_ref, acc_ref, state_ref, table_ref):
        self.own_cols, self.pad, self.radius = own_cols, pad, radius
        self.field_ref, self.take_ref, self.acc_ref = field_ref, take_ref, acc_ref
        self.state_ref, self.table_ref = state_ref, table_ref
        self.sub = lax.broadcasted_iota(jnp.int32, (SUBS, LANES), 0)
        self.lane = lax.broadcasted_iota(jnp.int32, (SUBS, LANES), 1)
        self.low = self.sub < HALF
        row = jnp.where(self.lane == 1, 4.0, jnp.where(self.lane < 3, 1.0, 0.0))
        self.ends = jnp.where((self.sub == 0) | (self.sub == HALF), row, 0.0)
        self.springs = self.ends * (END_STIFF / 36.0)
        self.zero = jnp.zeros((SUBS, LANES), jnp.float32)
        self.nothing = tuple((self.zero,) * 5 for _ in range(2))
        for h in range(2):
            first, second = POINTS[h], POINTS[3 - h]
            rows = (
                list(zip(cubic(first), cubic(second)))
                + list(zip(quadratic(first), quadratic(second)))
                + [(1.0 - first, 1.0 - second), (first, second)]
            )
            for i, (x, y) in enumerate(rows):
                table_ref[h, i] = jnp.where(self.low, jnp.float32(0.5 * x), jnp.float32(0.5 * y))

    def spread(self, source, offset, count):
        for c in range(source.shape[0] // (count * SUBS)):
            for i in range(count):
                start = (offset + i) * SUBS * SUBS + c
                row = (c * count + i) * SUBS
                self.field_ref[pl.ds(start, SUBS, stride=SUBS), :] = source[row : row + SUBS, :]

    def spread_rests(self, source, offset, count):
        chunk = source.shape[0] // (count * SUBS)
        for i in range(count):
            row = jnp.broadcast_to(source[i * SUBS + 7 : i * SUBS + 8, :], (SUBS, LANES))
            rests = pltpu.roll(row, LANES - FIRST_REST, 1, stride=REST, stride_axis=0)
            start = (offset + i) * SUBS * SUBS + chunk
            self.field_ref[pl.ds(start, SUBS, stride=SUBS), :] = jnp.where(
                self.lane < REST, rests, 0.0
            )

    def field(self, col, index):
        start = col * (SUBS * SUBS) + index * SUBS
        if not isinstance(start, int):
            start = pl.multiple_of(start, SUBS)
        return self.field_ref[pl.ds(start, SUBS), :]

    def shifted(self, v):
        following = pltpu.roll(v, SUBS - 1, 0)
        shifts = [v] + [
            pltpu.roll(jnp.where(self.lane < o, following, v), LANES - o, 1) for o in range(1, 4)
        ]
        return [jnp.where(self.low, z, pltpu.roll(z, HALF, 0)) for z in shifts]

    def value(self, z, h):
        return sum(self.table_ref[h, o] * z[o] for o in range(4))

    def slope(self, d, h):
        return sum(self.table_ref[h, 4 + o] * d[o] for o in range(3))

    def curve(self, g, h):
        return self.table_ref[h, 7] * g[0] + self.table_ref[h, 8] * g[1]

    def take_columns(self, cols, load, base, carry, thick=False):
        take_ref = self.take_ref

        def differences(z):
            return [z[o + 1] - z[o] for o in range(len(z) - 1)]

        loaded = [[load(col, i) for i in range(4 if thick else 3)] for col in cols]
        for col, vectors in zip(cols, loaded):
            za, zb, zc = (self.shifted(v) for v in vectors[:3])
            da, db, dc = differences(za), differences(zb), differences(zc)
            gc = differences(dc)
            zh = self.shifted(vectors[3]) if thick else None
            out = []
            for h in range(2):
                old_a0, old_b0, old_c0, old_c1, old_dc0 = carry[h]
                a0, b0, c0 = self.value(za, h), self.value(zb, h), self.value(zc, h)
                c1, dc0 = self.slope(dc, h), c0 - old_c0
                take_ref[base + A1, col, h] = self.slope(da, h)
                take_ref[base + B1, col, h] = self.slope(db, h)
                take_ref[base + C0, col, h] = c0
                take_ref[base + C1, col, h] = c1
                take_ref[base + DA0, col - 1, h] = a0 - old_a0
                take_ref[base + DB0, col - 1, h] = b0 - old_b0
                take_ref[base + DC0, col - 1, h] = dc0
                if thick:
                    take_ref[base + H0, col, h] = self.value(zh, h)
                else:
                    take_ref[base + C2, col, h] = self.curve(gc, h)
                    take_ref[base + DC1, col - 1, h] = c1 - old_c1
                    take_ref[base + DDC0, col - 2, h] = dc0 - old_dc0
                out.append((a0, b0, c0, c1, dc0))
            carry = tuple(out)
        return carry

    def axial_take(self, low, high, load, base, carry, thick=False, unroll=4):
        def body(cols, carry):
            return self.take_columns(cols, load, base, carry, thick)

        return loop(low, high, body, carry, unroll)

    def takes(self, name, k, h, taps):
        return [self.take_ref[name, k + o, h] for o in range(taps)]

    def prepare(self, low, high):
        inverse = 1.0 / (1.0 - POISSON * POISSON)
        takes, state_ref = self.takes, self.state_ref

        def body(cols, unused):
            (k,) = cols
            for h in range(2):
                u1 = take4(takes(A1, k, h, 4))
                us = take3(takes(DA0, k, h, 3))
                vs = take3(takes(DB0, k, h, 3))
                vx = take4(takes(B1, k, h, 4))
                w0 = take4(takes(C0, k, h, 4))
                w1 = take4(takes(C1, k, h, 4))
                ws = take3(takes(DC0, k, h, 3))
                h0 = take4(takes(H0, k, h, 4))
                for p in range(2):
                    t = POINTS[p]
                    weight = WEIGHTS[p] * WEIGHTS[h]
                    along = both(u1(t))
                    across = both(merged(vs(t), w0(t, 1.0 / self.radius)))
                    shear = both(merged(us(t), vx(t)))
                    tilt_x, tilt_s, thick = both(w1(t)), both(ws(t)), both(h0(t))
                    for q in range(2):
                        wx, wc, th = tilt_x[q], tilt_s[q], thick[q]
                        ex = along[q] + 0.5 * wx * wx
                        es = across[q] + 0.5 * wc * wc
                        g = shear[q] + wx * wc
                        a = th * (inverse * weight)
                        ag = a * (0.5 * (1.0 - POISSON))
                        point = p if q == 0 else 3 - p
                        state_ref[k, h, point, S_WX] = wx
                        state_ref[k, h, point, S_WS] = wc
                        state_ref[k, h, point, S_NX] = a * (ex + POISSON * es)
                        state_ref[k, h, point, S_NS] = a * (POISSON * ex + es)
                        state_ref[k, h, point, S_NG] = ag * g
                        state_ref[k, h, point, S_A] = a
                        state_ref[k, h, point, S_AG] = ag
                        state_ref[k, h, point, S_D] = a * (th * th) * (1.0 / 12.0)
            return unused

        loop(low, high, body, 0)

    def clear(self, low, count=None):
        for name, taps in TAPS:
            for o in range(taps - 1 if count is None else count):
                for h in range(2):
                    self.acc_ref[name, low + o, h] = self.zero

    def spans(self, low, high, fresh=True):
        takes, state_ref, acc_ref = self.takes, self.state_ref, self.acc_ref

        def add(name, k, h, parts):
            for o, part in enumerate(parts):
                if fresh and o == len(parts) - 1:
                    acc_ref[name, k + o, h] = part
                else:
                    acc_ref[name, k + o, h] += part

        def body(cols, unused):
            (k,) = cols
            for h in range(2):
                a1 = take4(takes(VECTOR + A1, k, h, 4))
                b1 = take4(takes(VECTOR + B1, k, h, 4))
                c0 = take4(takes(VECTOR + C0, k, h, 4))
                c1 = take4(takes(VECTOR + C1, k, h, 4))
                c2 = take4(takes(VECTOR + C2, k, h, 4))
                as0 = take3(takes(VECTOR + DA0, k, h, 3))
                bs0 = take3(takes(VECTOR + DB0, k, h, 3))
                cs0 = take3(takes(VECTOR + DC0, k, h, 3))
                cx0 = take3(takes(VECTOR + DC1, k, h, 3))
                cc0 = take2(takes(VECTOR + DDC0, k, h, 2))
                parts = []
                for p in range(2):
                    t = POINTS[p]
                    along = both(a1(t))
                    across = both(merged(bs0(t), c0(t, 1.0 / self.radius)))
                    shear = both(merged(as0(t), b1(t)))
                    tilt_x, tilt_s = both(c1(t)), both(cs0(t))
                    bend_x, bend_s = both(c2(t)), both(cc0(t))
                    twist = both(cx0(t, 2.0 * (1.0 - POISSON)))
                    results = []
                    for q in range(2):
                        point = p if q == 0 else 3 - p
                        wx, wc = state_ref[k, h, point, S_WX], state_ref[k, h, point, S_WS]
                        cx, cs = tilt_x[q], tilt_s[q]
                        ex = along[q] + wx * cx
                        es = across[q] + wc * cs
                        g = shear[q] + wx * cs + wc * cx
                        a = state_ref[k, h, point, S_A]
                        fx = a * (ex + POISSON * es)
                        fs = a * (POISSON * ex + es)
                        fg = state_ref[k, h, point, S_AG] * g
                        d = state_ref[k, h, point, S_D]
                        mx = d * (bend_x[q] + POISSON * bend_s[q])
                        ms = d * (POISSON * bend_x[q] + bend_s[q])
                        mg = d * twist[q]
                        ng = state_ref[k, h, point, S_NG]
                        sx = fx * wx + fg * wc + state_ref[k, h, point, S_NX] * cx + ng * cs
                        ss = fs * wc + fg * wx + state_ref[k, h, point, S_NS] * cs + ng * cx
                        results.append((fx, fs, fg, mx, ms, mg, sx, ss))
                    parts.append((t, list(zip(*results))))

                def pick(i):
                    return [(t, values[i]) for t, values in parts]

                add(F01, k, h, put4(pick(0)))
                add(F00, k, h, put3(pick(2)))
                add(F10, k, h, put3(pick(1)))
                add(F11, k, h, put4(pick(2)))
                add(F20, k, h, put4(pick(1), 1.0 / self.radius))
                add(F20Q, k, h, put3(pick(7)))
                add(F20L, k, h, put2(pick(4)))
                add(F21, k, h, put4(pick(6)))
                add(F21Q, k, h, put3(pick(5)))
                add(F22, k, h, put4(pick(3)))
            return unused

        loop(low, high, body, 0)

    def axial_put(self, zeroth, first, second):
        table_ref, lane, low = self.table_ref, self.lane, self.low
        t = [sum(table_ref[h, o] * zeroth[h] for h in range(2)) for o in range(4)]
        r = [sum(table_ref[h, 4 + o] * first[h] for h in range(2)) for o in range(3)]
        t = [t[0] - r[0], t[1] + (r[0] - r[1]), t[2] + (r[1] - r[2]), t[3] + r[2]]
        if second is not None:
            l0, l1 = (sum(table_ref[h, 7 + o] * second[h] for h in range(2)) for o in range(2))
            t = [t[0] + l0, t[1] + (l1 - 2.0 * l0), t[2] + (l0 - 2.0 * l1), t[3] + l1]
        return t

    def shifted_sums(self, items):
        lane, low = self.lane, self.low
        outs = []
        for i in range(0, len(items), 2):
            one, two = items[i], items[i + 1] if i + 1 < len(items) else None
            if two is None:
                packed = [x + pltpu.roll(x, HALF, 0) for x in one]
            else:
                packed = [
                    jnp.where(low, x, y) + pltpu.roll(jnp.where(low, y, x), HALF, 0)
                    for x, y in zip(one, two)
                ]
            stay, cross = packed[0], None
            for o in range(1, 4):
                moved = pltpu.roll(packed[o], o, 1)
                over = jnp.where(lane < o, moved, 0.0)
                stay = stay + jnp.where(lane < o, 0.0, moved)
                cross = over if cross is None else cross + over
            outs.append(jnp.where(low, stay, 0.0) + pltpu.roll(jnp.where(low, cross, 0.0), 1, 0))
            if two is not None:
                carried = pltpu.roll(jnp.where(low, 0.0, cross), HALF + 1, 0)
                outs.append(jnp.where(low, pltpu.roll(stay, HALF, 0), 0.0) + carried)
        return outs

    def end_parts(self, items):
        outs = []
        for i in range(0, len(items), HALF):
            group = items[i : i + HALF]
            rows = None
            for j, v in enumerate(group):
                row = v * self.ends if j == 0 else pltpu.roll(v * self.ends, j, 0)
                rows = row if rows is None else rows + row
            total = jnp.broadcast_to(jnp.sum(rows, axis=1, keepdims=True), (SUBS, LANES))
            for j in range(len(group)):
                turned = total if j == 0 else pltpu.roll(total, SUBS - j, 0)
                outs.append(turned * self.springs)
        return outs

    def line(self, name, column, h):
        return sum(MARKS[j] * self.take_ref[name, column + j, h] for j in range(3))

    def line_state(self, column, h):
        along, tilt = self.line(A1, column, h), self.line(C1, column, h)
        return along + 0.5 * tilt * tilt, tilt

    def stringer(self, column, states):
        for h in range(2):
            weight = jnp.float32(WEIGHTS[h])
            stretch, tilt = states[h]
            slope_c = self.line(VECTOR + C1, column, h)
            d_stretch = self.line(VECTOR + A1, column, h) + tilt * slope_c
            f0 = (STRINGER_AXIAL * weight) * d_stretch
            f1 = (STRINGER_AXIAL * weight) * (d_stretch * tilt + stretch * slope_c)
            f2 = (STRINGER_BENDING * weight) * self.line(VECTOR + C2, column, h)
            for j in range(3):
                self.acc_ref[F01, column + j, h] += MARKS[j] * f0
                self.acc_ref[F21, column + j, h] += MARKS[j] * f1
                self.acc_ref[F22, column + j, h] += MARKS[j] * f2

    def image_columns(self, cols, load):
        acc_ref, halves = self.acc_ref, range(2)

        def back(name, col, h):
            return acc_ref[name, col - 1, h] - acc_ref[name, col, h]

        work = []
        for col in cols:
            zeroth = [
                [back(F00, col, h) for h in halves],
                [back(F10, col, h) for h in halves],
                [
                    acc_ref[F20, col, h]
                    + back(F20Q, col, h)
                    + (acc_ref[F20L, col - 2, h] - acc_ref[F20L, col - 1, h])
                    - back(F20L, col, h)
                    for h in halves
                ],
            ]
            first = [
                [acc_ref[F01, col, h] for h in halves],
                [acc_ref[F11, col, h] for h in halves],
                [acc_ref[F21, col, h] + back(F21Q, col, h) for h in halves],
            ]
            second = [None, None, [acc_ref[F22, col, h] for h in halves]]
            work.append((zeroth, first, second, [load(col, i) for i in range(3)]))
        sums = self.shifted_sums(
            [self.axial_put(z[i], f[i], s[i]) for z, f, s, v in work for i in range(3)]
        )
        ends = self.end_parts([v[i] for z, f, s, v in work for i in range(3)])
        images = [x + y for x, y in zip(sums, ends)]
        return [images[i : i + 3] for i in range(0, len(images), 3)]

    def gather(self, low, high, load, image_ref, step, follow, carry, unroll, beyond=0):
        count = high - low
        ahead = min(count, unroll + count % unroll)

        def put(cols, images):
            for col, image in zip(cols, images):
                for i in range(3):
                    image_ref[step, col, i] = image[i]

        def body(start, carry):
            cols = [start + ahead + u for u in range(unroll)]
            carry = follow([start + u for u in range(unroll)], carry)
            put(cols, self.image_columns(cols, load))
            return carry

        cols = list(range(low, low + ahead))
        put(cols, self.image_columns(cols, load))
        rounds = (count - ahead) // unroll
        if rounds > 0:
            carry = lax.fori_loop(0, rounds, lambda i, c: body(low + i * unroll, c), carry)
        return follow(list(range(low + rounds * unroll, high + beyond)), carry)


def attached(source, shift):
    row = source[7:8, :]
    above = lax.broadcasted_iota(jnp.int32, row.shape, 1) >= ABOVE
    return jnp.max(jnp.where(above, row, 0.0)).astype(jnp.int32) + shift


def keep(ref, index, carry):
    for h in range(2):
        for i in range(5):
            ref[index, h, i] = carry[h][i]


def own_kernel(
    own_cols,
    pad,
    radius,
    own_ref,
    field_ref,
    take_ref,
    acc_ref,
    second_ref,
    state_ref,
    image_ref,
    carry_ref,
    table_ref,
):
    shell = Shell(own_cols, pad, radius, field_ref, take_ref, acc_ref, state_ref, table_ref)
    for col in range(pad, pad + own_cols):
        for i in range(3, 6):
            start = col * SUBS * SUBS + i * SUBS
            field_ref[start : start + SUBS, :] = shell.zero
    shell.spread(own_ref, pad, own_cols)
    stop = pad + own_cols
    shell.clear(pad - HALO, HALO)

    def state(col, index):
        return shell.field(col, (0, 1, 2, 6)[index])

    def direction(col, index):
        return shell.field(col, 3 + index)

    def image(col, index):
        return image_ref[0, col, index]

    keep(carry_ref, 0, shell.axial_take(pad, stop, state, 0, shell.nothing, thick=True))
    keep(carry_ref, 1, shell.axial_take(pad, stop, direction, VECTOR, shell.nothing))
    shell.prepare(pad, stop - 3)
    shell.clear(pad)
    shell.spans(pad, stop - 3)
    column = attached(own_ref, pad)
    shell.stringer(column, [shell.line_state(column, h) for h in range(2)])

    def follow(cols, carry):
        return shell.take_columns(cols, image, VECTOR, carry)

    carry = shell.gather(
        pad + 3, stop - 3, direction, image_ref, 0, follow, shell.nothing, unroll=3
    )
    keep(carry_ref, 2, carry)
    shell.acc_ref = second_ref
    shell.clear(pad + 3 - HALO, HALO)
    shell.clear(pad + 3)
    shell.spans(pad + 3, stop - 6)


def krylov_kernel(
    own_cols,
    pad,
    radius,
    left_ref,
    right_ref,
    own_ref,
    carry_ref,
    field_in,
    take_in,
    acc_in,
    second_in,
    state_in,
    image_in,
    krylov_ref,
    gram_ref,
    field_ref,
    take_ref,
    acc_ref,
    second_ref,
    state_ref,
    image_ref,
    table_ref,
    line_ref,
):
    shell = Shell(own_cols, pad, radius, field_ref, take_ref, acc_ref, state_ref, table_ref)
    field, zero = shell.field, shell.zero
    stop = pad + own_cols
    for source, offset in ((left_ref, pad - HALO), (right_ref, stop)):
        shell.spread(source, offset, HALO)
        shell.spread_rests(source, offset, HALO)

    def carried(index):
        return tuple(tuple(carry_ref[index, h, i] for i in range(5)) for h in range(2))

    def state(col, index):
        return field(col, (0, 1, 2, 6)[index])

    def vector(step):
        def load(col, index):
            if step == 0:
                return field(col, 3 + index)
            return image_ref[step - 1, col, index]

        return load

    shell.axial_take(pad - HALO, pad + 2, state, 0, shell.nothing, thick=True)
    shell.axial_take(stop, stop + HALO, state, 0, carried(0), thick=True)
    shell.prepare(pad - HALO, pad)
    shell.prepare(stop - 3, stop + HALO - 3)
    stringers = [
        attached(source, pad + (i - 1) * own_cols)
        for i, source in enumerate((left_ref, own_ref, right_ref))
    ]
    for i, column in enumerate(stringers):
        for h in range(2):
            line_ref[i, h, 0], line_ref[i, h, 1] = shell.line_state(column, h)

    def add_stringers(which):
        for i in which:
            shell.stringer(
                stringers[i], [(line_ref[i, h, 0], line_ref[i, h, 1]) for h in range(2)]
            )

    def take_next(step):
        load = vector(step + 1)
        return lambda cols, carry: shell.take_columns(cols, load, VECTOR, carry)

    def inner(cols, sums):
        sums = list(sums)
        for col in cols:
            for comp in range(3):
                vectors = [vector(s)(col, comp) for s in range(STEPS + 1)]
                for s, x in enumerate(vectors):
                    start = (col - pad) * (3 * SUBS) + comp * SUBS
                    if not isinstance(start, int):
                        start = pl.multiple_of(start, SUBS)
                    krylov_ref[s, pl.ds(start, SUBS), :] = x
                for n, (i, j) in enumerate(PAIRS):
                    sums[n] = sums[n] + vectors[i] * vectors[j]
        return tuple(sums)

    for step in range(STEPS):
        reach = HALO - 3 * step
        first, last = pad - reach, stop + reach - 3
        low, high = pad + 3 * step, stop - 3 * step
        load = vector(step)
        if step == 0:
            shell.axial_take(first, low + 2, load, VECTOR, shell.nothing)
            shell.axial_take(high, last + 3, load, VECTOR, carried(1))
        shell.acc_ref = second_ref if step == 1 else acc_ref
        if step < 2:
            shell.spans(first, low, fresh=False)
            shell.spans(high - 3, last)
        else:
            shell.clear(first)
            shell.spans(first, last)
        add_stringers((0, 2) if step == 0 else (0, 1, 2))
        if step == 0:
            follow = take_next(step)
            shell.gather(
                first + 3, low + 3, load, image_ref, step, follow, shell.nothing, 3, beyond=2
            )
            shell.gather(high - 3, last, load, image_ref, step, follow, carried(2), 3)
        elif step < STEPS - 1:
            follow = take_next(step)
            shell.gather(first + 3, last, load, image_ref, step, follow, shell.nothing, 4)
        else:
            nothing = (zero,) * len(PAIRS)
            sums = shell.gather(pad, stop, load, image_ref, step, inner, nothing, 4)

    row = jnp.zeros((1, LANES), jnp.float32)
    for n, s in enumerate(sums):
        part = jnp.sum(jnp.sum(s, axis=0, keepdims=True), axis=1, keepdims=True)
        row = jnp.where(shell.lane[0:1] == n, part, row)
    gram_ref[...] = jnp.broadcast_to(row, gram_ref.shape)


def combine_kernel(count_all, gram_ref, krylov_ref, vectors_ref, alpha_ref, beta_ref):
    row = jnp.sum(gram_ref[...], axis=0, keepdims=True) * (1.0 / count_all)
    gram = {}
    for n, (i, j) in enumerate(PAIRS):
        gram[i, j] = gram[j, i] = row[:, n : n + 1]

    def product(x, y):
        return sum(x[i] * (sum(gram[i, j] * y[j] for j in range(len(y)))) for i in range(len(x)))

    def raised(x):
        return [jnp.zeros_like(x[0])] + x

    def less(x, scale, y):
        return [
            x[i] - scale * y[i] if i < len(y) else x[i] for i in range(len(x))
        ]

    current = [jnp.ones((1, 1), jnp.float32)]
    previous = None
    square = product(current, current) + EPSILON
    scale = square
    alphas, polynomials, scales, betas = [], [], [], []
    for step in range(STEPS):
        image = raised(current)
        alpha = product(current, image) / scale
        following = less(image, alpha, current)
        if previous is not None:
            following = less(following, square, previous)
        previous, current = current, following
        square = product(current, current) / scale + EPSILON
        scale = scale * square
        alphas.append(alpha)
        betas.append(square)
        polynomials.append(current)
        scales.append(scale)
    root = jnp.sqrt(jnp.concatenate(betas, axis=0))
    inverse = [1.0 / jnp.sqrt(s) for s in scales]
    for s in range(STEPS):
        alpha_ref[s] = jnp.max(alphas[s])
        beta_ref[s] = jnp.max(root[s : s + 1, :])
    factors = [
        [jnp.broadcast_to(c * inverse[s], (SUBS, LANES)) for c in polynomials[s]]
        for s in range(STEPS)
    ]
    own_cols, length = vectors_ref.shape[2], vectors_ref.shape[3]
    for comp in range(3):
        for block in range(own_cols // SUBS):
            for c in range((length + LANES - 1) // LANES):
                start = block * SUBS * 3 * SUBS + comp * SUBS + c
                vectors = [
                    krylov_ref[s, pl.ds(start, SUBS, stride=3 * SUBS), :] for s in range(STEPS + 1)
                ]
                width = min(LANES, length - c * LANES)
                for s in range(STEPS):
                    result = sum(factors[s][i] * vectors[i] for i in range(s + 2))
                    vectors_ref[
                        s, comp, block * SUBS : (block + 1) * SUBS, c * LANES : c * LANES + width
                    ] = result[:, :width]


def per_device(state_field, direction, skin_thickness, stringer_column):
    count = lax.axis_size("circ")
    own_cols, axial_count = state_field.shape[1:]
    radius = own_cols * count / (2.0 * math.pi)
    count_all = 3.0 * own_cols * axial_count * count
    pad = own_cols
    chunks = -(-axial_count // LANES)
    columns = 3 * own_cols
    vmem = pl.BlockSpec(memory_space=pltpu.VMEM)
    smem = pl.BlockSpec(memory_space=pltpu.SMEM)

    def shape(*dims):
        return jax.ShapeDtypeStruct(dims, jnp.float32)

    def params(mebibytes):
        return pltpu.CompilerParams(vmem_limit_bytes=mebibytes * 1024 * 1024)

    fields = jnp.concatenate([state_field, direction, skin_thickness[None]], axis=0)
    packed, head, tail = pl.pallas_call(
        functools.partial(pack_kernel, own_cols),
        out_shape=(
            shape(chunks * own_cols * SUBS, LANES),
            shape((chunks - 1) * HALO * SUBS, LANES),
            shape((chunks - 1) * HALO * SUBS, LANES),
        ),
        in_specs=[vmem, smem],
        out_specs=(vmem,) * 3,
        compiler_params=params(8),
        name="pack",
    )(fields, stringer_column)
    left = lax.ppermute(tail, "circ", [(i, (i + 1) % count) for i in range(count)])
    right = lax.ppermute(head, "circ", [((i + 1) % count, i) for i in range(count)])
    buffers = (
        shape(columns * SUBS * SUBS, LANES),
        shape(21, columns, 2, SUBS, LANES),
        shape(10, columns, 2, SUBS, LANES),
        shape(10, columns, 2, SUBS, LANES),
        shape(columns, 2, 4, 8, SUBS, LANES),
        shape(STEPS, columns, 3, SUBS, LANES),
    )
    table = pltpu.VMEM((2, 9, SUBS, LANES), jnp.float32)
    *kept, carry = pl.pallas_call(
        functools.partial(own_kernel, own_cols, pad, radius),
        out_shape=buffers + (shape(3, 2, 5, SUBS, LANES),),
        in_specs=[vmem],
        out_specs=(vmem,) * 7,
        scratch_shapes=[table],
        compiler_params=params(4),
        cost_estimate=pl.CostEstimate(flops=40000000, bytes_accessed=20000000, transcendentals=0),
        name="own",
    )(packed)
    krylov, gram, *_ = pl.pallas_call(
        functools.partial(krylov_kernel, own_cols, pad, radius),
        out_shape=(shape(STEPS + 1, own_cols * 3 * SUBS, LANES), shape(count, LANES)) + buffers,
        in_specs=[vmem] * 10,
        out_specs=(vmem,) * 8,
        input_output_aliases={4 + i: 2 + i for i in range(len(buffers))},
        scratch_shapes=[
            table,
            pltpu.VMEM((3, 2, 2, SUBS, LANES), jnp.float32),
        ],
        compiler_params=params(8),
        name="krylov",
    )(left, right, packed, carry, *kept)
    gram = lax.all_to_all(gram, "circ", 0, 0, tiled=True)
    return pl.pallas_call(
        functools.partial(combine_kernel, count_all),
        out_shape=(shape(STEPS, 3, own_cols, axial_count), shape(STEPS), shape(STEPS)),
        in_specs=[vmem] * 2,
        out_specs=(vmem, smem, smem),
        compiler_params=params(8),
        name="combine",
    )(gram, krylov)


def solution(mesh):
    in_specs = (P("group", "circ", None), P("group", "circ", None), P("circ", None), P("circ"))
    out_specs = (P("group", None, "circ", None), P("group"), P("group"))
    return jax.shard_map(
        per_device, mesh=mesh, in_specs=in_specs, out_specs=out_specs, check_vma=False
    )
```
